32 devices in a mesh: shot: 16 (over z, y, x), tm: 2 (over core).
Axes of the slice: x: 2, y: 2, z: 4, core: 2. Of those that a mesh axis runs over, the one named last changes fastest.
Arguments:
- shot_data: float32 [32, 512, 256], P('shot', None, 'tm'), may hold values from -6 to 6
- live_mask: int32 [32, 512], P('shot'), may hold values 0 or 1
- recv_order: int32 [512], replicated, may hold values from 0 to 511, each once
- rec_taps: float32 [31], replicated, may hold values from -1 to 1
- time_taps: float32 [31], replicated, may hold values from -1 to 1
- shot_taps: float32 [31], replicated, may hold values from -1 to 1
- late_taps: float32 [31], replicated, may hold values from -1 to 1
Outputs:
- filtered: float32 [32, 512, 256], P(None, 'shot', 'tm')
The draws below stay inside these ranges and needn't reach their ends.
Inputs may be any that keep to these rules, and one draw needn't show every extreme that they name: `recv_order`: each station appears once.
All inputs are finite; a program needn't handle non-finite values. No bound on the sum of `live_mask` on one device may be relied on, other than what follows from the above.
Results may differ from the reference program's by a relative error of at most 0.00007.
Values sent between devices are 32-bit elements; how exact they have to be, the bound alone decides.
No kernel may reach another device: no remote copies, remote signals or barrier semaphores. Data moves between devices by JAX's collectives and lax.ppermute only.
A program may use at most 64 MiB of HBM per device.

```python
import jax
import jax.numpy as jnp
from jax import lax

TAPS = 31
SHOTS = 32
RECS = 512
NT = 256


def with_ends(result, key, smallest, top_value):
    longest = result.shape.index(max(result.shape))
    spots = []
    for shift in (0, 1):
        where = [jax.random.randint(jax.random.fold_in(key, axis), (), 0, length) for axis, length in enumerate(result.shape)]
        where[longest] = (where[longest] + shift) % result.shape[longest]
        spots.append(tuple(where))
    return result.at[spots[0]].set(smallest).at[spots[1]].set(top_value)


def level_of(key, shape, split, least, high):
    level, own = 1.0, jax.random.fold_in(key, 6)
    for dim, shards_of in split:
        draws = jnp.exp(jax.random.uniform(jax.random.fold_in(own, dim), (shards_of,), jnp.float32, least / len(split), high / len(split)))
        level = level * jnp.repeat(draws, shape[dim] // shards_of).reshape([-1 if axis == dim else 1 for axis in range(len(shape))])
    return level


def gaussian(own_key, shape, deviation, reach, pieces=(), dtype=jnp.bfloat16):
    loudness = level_of(own_key, shape, pieces, -0.22, 0.18) if pieces else 1.0
    drawn = jax.random.normal(own_key, shape, jnp.float32) * deviation * loudness
    return jnp.minimum(jnp.maximum(drawn, -reach), reach).astype(dtype)


def setup_inputs(seed: int = 0) -> dict:
    key_of = jax.random.split(jax.random.key(seed), 8)
    return {
        "shot_data": gaussian(key_of[0], (SHOTS, RECS, NT), 1.0, 6.0, ((0, 16), (2, 2)), jnp.float32),
        "live_mask": with_ends((jax.random.randint(key_of[1], (SHOTS, RECS), 0, 4) < 3).astype(jnp.int32), jax.random.fold_in(key_of[1], 1), 0, 1),
        "recv_order": jax.random.permutation(key_of[2], RECS).astype(jnp.int32),
        "rec_taps": gaussian(key_of[3], (TAPS,), TAPS ** -0.5, 1.0, (), jnp.float32),
        "time_taps": gaussian(key_of[4], (TAPS,), TAPS ** -0.5, 1.0, (), jnp.float32),
        "shot_taps": gaussian(key_of[5], (TAPS,), TAPS ** -0.5, 1.0, (), jnp.float32),
        "late_taps": gaussian(key_of[6], (TAPS,), TAPS ** -0.5, 1.0, (), jnp.float32),
    }


def slide_filter(values, tap_list, along):
    tap_count = tap_list.shape[0]
    half_width = (tap_count - 1) // 2
    extent = values.shape[along]
    config = [(0, 0)] * values.ndim
    config[along] = (half_width, half_width)
    padded = jnp.pad(values, config)
    summed = jnp.zeros(values.shape, jnp.float32)
    for offset in range(tap_count):
        summed = summed + tap_list[offset] * lax.slice_in_dim(padded, offset, offset + extent, axis=along)
    return summed


def reference(shot_data, live_mask, recv_order, rec_taps, time_taps, shot_taps, late_taps):
    alive_all = live_mask.astype(jnp.float32)

    def shot_pass(pair):
        traces, alive = pair
        masked = traces * alive[:, None]
        masked = slide_filter(masked, time_taps, 1)
        masked = slide_filter(masked, rec_taps, 0)
        return masked * alive[:, None]

    first = lax.map(shot_pass, (shot_data, alive_all))
    resorted = jnp.take(first, recv_order.astype(jnp.int32), axis=1)
    resorted = slide_filter(resorted, shot_taps, 0)
    return slide_filter(resorted, late_taps, 2)
```

```python
import functools

import jax
import jax.numpy as jnp
from jax import lax
from jax.experimental import pallas as pl
from jax.experimental.pallas import tpu as pltpu
from jax.sharding import PartitionSpec as P

LANES = 128
SUBLANES = 8
PIECES = 2
SORTED = 3
EXACT = lax.Precision.HIGHEST
VMEM = pl.BlockSpec(memory_space=pltpu.VMEM)
HBM = pl.BlockSpec(memory_space=pltpu.HBM)
SMEM = pl.BlockSpec(memory_space=pltpu.SMEM)


def iota(shape, dim):
    return lax.broadcasted_iota(jnp.int32, shape, dim)


def band(chunks, rows, cols, shift):
    blocks = []
    for start in range(0, cols, LANES):
        offset = iota((rows, LANES), 1) - iota((rows, LANES), 0) + (shift + start)
        block = None
        turn = jnp.asarray(-(shift + start), jnp.int32) & (LANES - 1)
        for q, chunk in enumerate(chunks):
            first = pltpu.roll(jnp.broadcast_to(chunk, (SUBLANES, LANES)), turn, 1)
            spread = pltpu.roll(
                jnp.broadcast_to(first[:1], (rows, LANES)), 0, 1, stride=1, stride_axis=0
            )
            here = (offset >= q * LANES) & (offset < (q + 1) * LANES)
            part = jnp.where(here, spread, 0.0)
            block = part if block is None else block + part
        blocks.append(block)
    return blocks[0] if len(blocks) == 1 else jnp.concatenate(blocks, axis=1)


def wide(ref, scratch):
    scratch[...] = jnp.zeros_like(scratch)
    scratch[0:1, 0 : ref.shape[1]] = ref[...]
    return scratch[0:1, :]


def dot(a, b):
    return jnp.dot(a, b, precision=EXACT, preferred_element_type=jnp.float32)


def dot_t(a, b):
    return lax.dot_general(
        a, b, (((1,), (1,)), ((), ())), precision=EXACT, preferred_element_type=jnp.float32
    )


def time_kernel(shifts, windows, time_ref, late_ref, x_ref, partial_ref, others_ref, scratch):
    shots, stations, window = x_ref.shape
    half = (time_ref.shape[1] - 1) // 2
    place = lax.axis_index("tm")
    base = window // 2
    late = band([wide(late_ref, scratch)], window, 2 * window, half - base)
    sample = place * window - base + iota((window, 2 * window), 1)
    late = jnp.where((sample >= 0) & (sample < windows * window), late, 0.0)
    taps = wide(time_ref, scratch)
    for n, shift in enumerate((lambda _: 0,) + shifts):
        matrix = dot(late, band([taps], 2 * window, window, shift(place) * window + base + half))
        if n == 0:
            own = dot_t(x_ref[...].reshape(shots * stations, window), matrix)
            partial_ref[...] = own.reshape(partial_ref.shape)
        else:
            others_ref[n - 1] = matrix


def station_kernel(order_ref, rec_ref, live_ref, partial_ref, matrix_ref, *refs):
    *halo_refs, out_ref, scratch, flags, padded, done = refs
    shots, stations, window = partial_ref.shape
    half = (rec_ref.shape[1] - 1) // 2
    flags[0:shots, :] = live_ref[...].astype(jnp.float32)
    columns = jnp.transpose(flags[...])
    edge = LANES // 2
    padded[0:edge, :] = jnp.zeros((edge, shots * window), jnp.float32)
    padded[edge + stations :, :] = jnp.zeros((edge, shots * window), jnp.float32)
    alive = [jnp.broadcast_to(columns[:, s : s + 1], (stations, window)) for s in range(shots)]
    for s in range(shots):
        total = partial_ref[s]
        for n, halo in enumerate(halo_refs):
            total = total + dot_t(halo[s], matrix_ref[n])
        padded[edge : edge + stations, s * window : (s + 1) * window] = total * alive[s]
    matrix = band([wide(rec_ref, scratch)], LANES, 2 * LANES, half - edge)
    for start in range(0, stations, LANES):
        block = dot(matrix, padded[start : start + 2 * LANES, :])
        for s in range(shots):
            done[s, start : start + LANES, :] = (
                block[:, s * window : (s + 1) * window] * alive[s][start : start + LANES]
            )
    groups, _, members, _ = out_ref.shape

    def group(g, carry):
        for q in range(members):
            station = order_ref[g * members + q]
            for s in range(shots):
                out_ref[g, s, pl.ds(q, 1), :] = done[s, pl.ds(station, 1), :]
        return carry

    lax.fori_loop(0, groups, group, 0)


def shot_matrix_kernel(half, taps_ref, out_ref):
    size = out_ref.shape[0]
    chunks = [taps_ref[q : q + 1, :] for q in range(taps_ref.shape[0])]
    out_ref[...] = band(chunks, size, size, SUBLANES * half)


def shot_kernel(matrix_ref, in_ref, out_ref):
    shots, members, window = in_ref.shape
    rows = SUBLANES * shots
    for start in range(0, members, 2 * SUBLANES):
        parts = [
            in_ref[:, a : a + SUBLANES, :].reshape(rows, window)
            for a in (start, start + SUBLANES)
        ]
        result = dot(matrix_ref[...], jnp.concatenate(parts, axis=1))
        for n, a in enumerate((start, start + SUBLANES)):
            out_ref[:, a : a + SUBLANES, :] = result[:, n * window : (n + 1) * window].reshape(
                shots, SUBLANES, window
            )


def split(value, count=2):
    pieces = []
    for _ in range(count):
        pieces.append(value.astype(jnp.bfloat16))
        if len(pieces) < count:
            value = value - pieces[-1].astype(jnp.float32)
    return pieces


def product(a, b):
    terms = ((0, 0), (1, 0), (0, 1))
    return sum(jnp.dot(a[i], b[j], preferred_element_type=jnp.float32) for i, j in terms)


def diagonal(ref, scratch, backwards):
    count = ref.shape[1]
    lane = iota((SUBLANES, LANES), 1) - iota((SUBLANES, LANES), 0)
    used = (lane >= 0) & (lane < count)
    lane = jnp.clip(lane, 0, count - 1)
    taps = jnp.broadcast_to(wide(ref, scratch), (SUBLANES, LANES))
    taps = jnp.take_along_axis(
        taps, count - 1 - lane if backwards else lane, axis=1, mode="promise_in_bounds"
    )
    pieces = split(jnp.where(used, taps, 0.0))
    return [piece.astype(jnp.float32) for piece in pieces], count + SUBLANES - 1


def banded(diagonals, rows, cols, first, mask=None):
    pieces, wide_lanes = diagonals
    lane = iota((SUBLANES, LANES), 1)
    strips = [[] for _ in pieces]
    for row in range(0, rows, SUBLANES):
        start = row + first
        stop = start + wide_lanes
        for n, piece in enumerate(pieces):
            turned = pltpu.roll(piece, start % LANES, 1)
            tiles = []
            for low in range(0, cols, LANES):
                high = low + LANES
                if stop <= low or start >= high:
                    tiles.append(jnp.zeros((SUBLANES, LANES), jnp.float32))
                    continue
                tile = turned
                if start < low:
                    tile = jnp.where(lane < stop - low, tile, 0.0)
                elif stop > high:
                    tile = jnp.where(lane >= start - low, tile, 0.0)
                if mask is not None:
                    tile = tile * mask[:, low:high]
                tiles.append(tile)
            strips[n].append(jnp.concatenate(tiles, axis=1))
    return [jnp.concatenate(parts, axis=0).astype(jnp.bfloat16) for parts in strips]


MARGIN = LANES // 2
REACH = 2 * LANES


def spans(stations):
    step = REACH - 2 * MARGIN
    return [(start, min(step, stations - start)) for start in range(0, stations, step)]


def prepare_kernel(
    time_hbm, late_hbm, rec_hbm, shot_hbm, live_hbm, order_hbm, data_hbm, *refs
):
    times_ref, stations_ref, order_ref, own_ref, across_ref, *refs = refs
    time_ref, late_ref, rec_ref, shot_ref, live_ref, place_ref, data_ref, scratch, flags, sems = refs
    place = lax.axis_index("tm")
    stations, window = data_ref.shape
    samples = 2 * window
    half = (time_ref.shape[1] - 1) // 2
    pairs = (
        (time_hbm, time_ref),
        (late_hbm, late_ref),
        (rec_hbm, rec_ref),
        (shot_hbm, shot_ref),
        (live_hbm, live_ref),
        (order_hbm, place_ref),
        (data_hbm.at[place], data_ref),
    )
    copies = [pltpu.make_async_copy(a, b, sems.at[n]) for n, (a, b) in enumerate(pairs)]
    for copy in copies:
        copy.start()
    flags[...] = jnp.zeros_like(flags)
    for copy in copies[:6]:
        copy.wait()
    time_pieces = banded(diagonal(time_ref, scratch.at[0], True), samples, samples, -half)
    late_pieces = banded(diagonal(late_ref, scratch.at[1], True), samples, samples, -half)
    both = split(product(time_pieces, late_pieces))
    for n, piece in enumerate(both):
        for side in range(2):
            row = pl.multiple_of((place ^ side) * window, window)
            times_ref[n, pl.ds(row, window), :] = piece[side * window : (side + 1) * window, :]
    alive = live_ref[pl.ds(place, 1), :].astype(jnp.float32)
    flags[0:1, MARGIN : MARGIN + stations] = alive
    taps = diagonal(rec_ref, scratch.at[2], False)
    for m, (start, count) in enumerate(spans(stations)):
        mask = jnp.broadcast_to(flags[0:1, start : start + REACH], (SUBLANES, REACH))
        for n, piece in enumerate(banded(taps, count, REACH, MARGIN - half, mask)):
            stations_ref[n, m, 0:count, :] = piece
    order = jnp.broadcast_to(place_ref[...].astype(jnp.float32), (SUBLANES, stations))
    order = jnp.transpose(order)[:, 0:1]
    numbers = iota((stations, stations), 1).astype(jnp.float32)
    order_ref[...] = jnp.where(numbers == order, alive, 0.0).astype(jnp.bfloat16)
    copies[6].wait()
    for n, piece in enumerate(split(data_ref[...])):
        own_ref[n] = piece
    matrix = spread_matrix(shot_ref, scratch.at[3], across_ref.shape[1] // SUBLANES)
    for n, piece in enumerate(matrix):
        across_ref[n] = piece


def sorted_kernel(times_ref, stations_ref, order_ref, own_ref, other_ref, out_ref, *refs):
    padded, done = refs
    place = lax.axis_index("tm")
    _, stations, window = other_ref.shape
    tail = padded.shape[1] - MARGIN - stations
    padded[:, 0:MARGIN, :] = jnp.zeros((PIECES, MARGIN, 2 * window), jnp.bfloat16)
    padded[:, MARGIN + stations :, :] = jnp.zeros((PIECES, tail, 2 * window), jnp.bfloat16)
    other = split(other_ref[place])
    both = [jnp.concatenate([own_ref[n], other[n]], axis=1) for n in range(PIECES)]
    times = [times_ref[n] for n in range(PIECES)]
    step = stations // 2
    for start in range(0, stations, step):
        filtered = product([piece[start : start + step] for piece in both], times)
        for n, piece in enumerate(split(filtered)):
            padded[n, MARGIN + start : MARGIN + start + step, :] = piece
    for m, (start, count) in enumerate(spans(stations)):
        taps = [stations_ref[n, m, 0:count, :] for n in range(PIECES)]
        block = product(taps, [padded[n, start : start + REACH, :] for n in range(PIECES)])
        for n, piece in enumerate(split(block, SORTED)):
            done[n, start : start + count, :] = piece
    groups, _, members, _ = out_ref.shape
    step = groups // 2
    for first in range(0, groups, step):
        pick = order_ref[first * members : (first + step) * members, :]
        rows = sum(
            jnp.dot(pick, done[n], preferred_element_type=jnp.float32)
            for n in reversed(range(SORTED))
        )
        for side in range(2):
            out_ref[first : first + step, side] = rows[
                :, side * window : (side + 1) * window
            ].reshape(step, members, window)


def spread_matrix(ref, scratch, shots):
    count = ref.shape[1]
    half = (count - 1) // 2
    lane = iota((SUBLANES, LANES), 1)
    turn = lane - iota((SUBLANES, LANES), 0)
    taps = jnp.broadcast_to(wide(ref, scratch), (SUBLANES, LANES))
    chunks = []
    for low in range(0, SUBLANES * count, LANES):
        at = turn + low
        used = (at >= 0) & (at < SUBLANES * count) & (at & (SUBLANES - 1) == 0)
        tap = jnp.clip(at >> (SUBLANES.bit_length() - 1), 0, count - 1)
        picked = jnp.take_along_axis(taps, tap, axis=1, mode="promise_in_bounds")
        chunks.append([p.astype(jnp.float32) for p in split(jnp.where(used, picked, 0.0))])
    none = jnp.zeros((SUBLANES, LANES), jnp.float32)
    strips = [[] for _ in range(PIECES)]
    for shot in range(shots):
        start = SUBLANES * (shot - half)
        for n in range(PIECES):
            turned = [pltpu.roll(chunk[n], start % LANES, 1) for chunk in chunks]
            tiles = []
            for low in range(0, SUBLANES * shots, LANES):
                tile = none
                for q in range(len(chunks)):
                    at = start + q * LANES - low
                    if at == 0:
                        tile = turned[q]
                    elif 0 < at < LANES:
                        tile = jnp.where(lane >= at, turned[q], tile)
                    elif -LANES < at < 0:
                        tile = jnp.where(lane < at + LANES, turned[q], tile)
                tiles.append(tile)
            strips[n].append(jnp.concatenate(tiles, axis=1))
    return [jnp.concatenate(parts, axis=0).astype(jnp.bfloat16) for parts in strips]


def across_kernel(matrix_ref, in_ref, out_hbm, result, sems):
    shots, members, window = in_ref.shape
    matrix = [matrix_ref[n] for n in range(PIECES)]
    copies = []
    for start in range(0, members, 2 * SUBLANES):
        parts = [
            in_ref[:, a : a + SUBLANES, :].reshape(SUBLANES * shots, window)
            for a in (start, start + SUBLANES)
        ]
        rows = product(matrix, split(jnp.concatenate(parts, axis=1)))
        for n, a in enumerate((start, start + SUBLANES)):
            result[:, a : a + SUBLANES, :] = rows[:, n * window : (n + 1) * window].reshape(
                shots, SUBLANES, window
            )
        span = (slice(None), pl.ds(start, 2 * SUBLANES))
        copies.append(
            pltpu.make_async_copy(result.at[span], out_hbm.at[span], sems.at[len(copies)])
        )
        copies[-1].start()
    for copy in copies:
        copy.wait()


def still(array):
    return pltpu.with_memory_space_constraint(array, pltpu.HBM)


def paired(shot_data, live_mask, recv_order, rec_taps, time_taps, shot_taps, late_taps):
    shots, stations, window = shot_data.shape
    groups = lax.axis_size("shot")
    members = stations // groups
    f32, bf16 = jnp.float32, jnp.bfloat16
    row = lambda values: values.reshape(1, -1)
    samples = 2 * window
    blocks = spans(stations)
    tap_count = rec_taps.shape[0]
    grant = pltpu.CompilerParams(vmem_limit_bytes=16 * 2**20)
    traded = lax.ppermute(shot_data, "tm", [(0, 1), (1, 0)])
    taps = [row(values) for values in (time_taps, late_taps, rec_taps, shot_taps)]
    total_shots = groups * shots
    spread = SUBLANES * total_shots
    *prepared, matrix = pl.pallas_call(
        prepare_kernel,
        out_shape=[
            jax.ShapeDtypeStruct((PIECES, samples, samples), bf16),
            jax.ShapeDtypeStruct((PIECES, len(blocks), REACH - 2 * MARGIN, REACH), bf16),
            jax.ShapeDtypeStruct((stations, stations), bf16),
            jax.ShapeDtypeStruct((PIECES, stations, window), bf16),
            jax.ShapeDtypeStruct((PIECES, spread, spread), bf16),
        ],
        in_specs=[HBM] * 7,
        out_specs=[VMEM] * 5,
        scratch_shapes=[pltpu.VMEM((1, tap_count), f32)] * 4
        + [
            pltpu.VMEM((shots, stations), jnp.int32),
            pltpu.VMEM((1, stations), jnp.int32),
            pltpu.VMEM((stations, window), f32),
            pltpu.VMEM((4, SUBLANES, LANES), f32),
            pltpu.VMEM((1, blocks[-1][0] + REACH), f32),
            pltpu.SemaphoreType.DMA((7,)),
        ],
        compiler_params=grant,
        cost_estimate=pl.CostEstimate(flops=10**8, bytes_accessed=10**6, transcendentals=0),
    )(*(still(a) for a in (*taps, live_mask, row(recv_order), shot_data)))
    packed = pl.pallas_call(
        sorted_kernel,
        out_shape=jax.ShapeDtypeStruct((groups, 2, members, window), f32),
        in_specs=[VMEM] * 5,
        out_specs=VMEM,
        scratch_shapes=[
            pltpu.VMEM((PIECES, blocks[-1][0] + REACH, samples), bf16),
            pltpu.VMEM((SORTED, stations, samples), bf16),
        ],
        compiler_params=grant,
    )(*prepared, traded)
    packed = packed.reshape(groups * 2, members, window)
    moved = lax.all_to_all(packed, ("shot", "tm"), split_axis=0, concat_axis=0, tiled=True)
    return pl.pallas_call(
        across_kernel,
        out_shape=jax.ShapeDtypeStruct(moved.shape, f32),
        in_specs=[VMEM] * 2,
        out_specs=HBM,
        scratch_shapes=[
            pltpu.VMEM(moved.shape, f32),
            pltpu.SemaphoreType.DMA((members // (2 * SUBLANES),)),
        ],
        compiler_params=grant,
    )(matrix, moved)


def spread_taps(taps):
    spread = lax.pad(taps, jnp.float32(0), [(0, 0, SUBLANES - 1)])
    return jnp.pad(spread, (0, -spread.shape[0] % LANES)).reshape(-1, LANES)


def shards(shot_data, live_mask, recv_order, rec_taps, time_taps, shot_taps, late_taps):
    shots, stations, window = shot_data.shape
    windows = lax.axis_size("tm")
    groups = lax.axis_size("shot")
    if windows == 2 and shots == 2:
        return paired(
            shot_data, live_mask, recv_order, rec_taps, time_taps, shot_taps, late_taps
        )
    f32 = jnp.float32
    up = [(i, i + 1) for i in range(windows - 1)]
    down = [(j, i) for i, j in up]
    halos = [lax.ppermute(shot_data, "tm", up), lax.ppermute(shot_data, "tm", down)]
    shifts = (lambda place: -1, lambda place: 1)
    row = lambda taps: taps.reshape(1, -1)
    partial, matrices = pl.pallas_call(
        functools.partial(time_kernel, shifts, windows),
        out_shape=[
            jax.ShapeDtypeStruct((shots, stations, window), f32),
            jax.ShapeDtypeStruct((len(halos), window, window), f32),
        ],
        compiler_params=pltpu.CompilerParams(vmem_limit_bytes=32 * 2**20),
        in_specs=[VMEM] * 3,
        out_specs=[VMEM] * 2,
        scratch_shapes=[pltpu.VMEM((SUBLANES, LANES), f32)],
        cost_estimate=pl.CostEstimate(flops=10**8, bytes_accessed=10**6, transcendentals=0),
    )(row(time_taps), row(late_taps), shot_data)
    members = stations // groups
    blocks = pl.pallas_call(
        station_kernel,
        out_shape=jax.ShapeDtypeStruct((groups, shots, members, window), f32),
        compiler_params=pltpu.CompilerParams(vmem_limit_bytes=32 * 2**20),
        in_specs=[SMEM] + [VMEM] * (4 + len(halos)),
        out_specs=VMEM,
        scratch_shapes=[
            pltpu.VMEM((SUBLANES, LANES), f32),
            pltpu.VMEM((SUBLANES, stations), f32),
            pltpu.VMEM((stations + LANES, shots * window), f32),
            pltpu.VMEM((shots, stations, window), f32),
        ],
    )(recv_order, row(rec_taps), live_mask, partial, matrices, *halos)
    moved = lax.all_to_all(blocks, "shot", split_axis=0, concat_axis=0, tiled=True)
    total_shots = groups * shots
    moved = moved.reshape(total_shots, members, window)
    matrix = pl.pallas_call(
        functools.partial(shot_matrix_kernel, (shot_taps.shape[0] - 1) // 2),
        out_shape=jax.ShapeDtypeStruct((SUBLANES * total_shots, SUBLANES * total_shots), f32),
        compiler_params=pltpu.CompilerParams(vmem_limit_bytes=32 * 2**20),
        in_specs=[VMEM],
        out_specs=VMEM,
        cost_estimate=pl.CostEstimate(flops=10**6, bytes_accessed=10**6, transcendentals=0),
    )(spread_taps(shot_taps))
    return pl.pallas_call(
        shot_kernel,
        out_shape=jax.ShapeDtypeStruct(moved.shape, f32),
        compiler_params=pltpu.CompilerParams(vmem_limit_bytes=32 * 2**20),
        in_specs=[VMEM] * 2,
        out_specs=VMEM,
    )(matrix, moved)


def solution(mesh):
    placed = (P("shot", None, "tm"), P("shot", None), P(), P(), P(), P(), P())
    return jax.shard_map(
        shards, mesh=mesh, in_specs=placed, out_specs=P(None, "shot", "tm"), check_vma=False
    )
```

```python
import functools

import jax
import jax.numpy as jnp
from jax import lax
from jax.experimental import pallas as pl
from jax.experimental.pallas import tpu as pltpu
from jax.sharding import PartitionSpec as P

LANES = 128
SUBLANES = 8
PIECES = 3
SORTED = 3
EXACT = lax.Precision.HIGHEST
VMEM = pl.BlockSpec(memory_space=pltpu.VMEM)
HBM = pl.BlockSpec(memory_space=pltpu.HBM)
SMEM = pl.BlockSpec(memory_space=pltpu.SMEM)


def iota(shape, dim):
    return lax.broadcasted_iota(jnp.int32, shape, dim)


def band(chunks, rows, cols, shift):
    blocks = []
    for start in range(0, cols, LANES):
        offset = iota((rows, LANES), 1) - iota((rows, LANES), 0) + (shift + start)
        block = None
        turn = jnp.asarray(-(shift + start), jnp.int32) & (LANES - 1)
        for q, chunk in enumerate(chunks):
            first = pltpu.roll(jnp.broadcast_to(chunk, (SUBLANES, LANES)), turn, 1)
            spread = pltpu.roll(
                jnp.broadcast_to(first[:1], (rows, LANES)), 0, 1, stride=1, stride_axis=0
            )
            here = (offset >= q * LANES) & (offset < (q + 1) * LANES)
            part = jnp.where(here, spread, 0.0)
            block = part if block is None else block + part
        blocks.append(block)
    return blocks[0] if len(blocks) == 1 else jnp.concatenate(blocks, axis=1)


def wide(ref, scratch):
    scratch[...] = jnp.zeros_like(scratch)
    scratch[0:1, 0 : ref.shape[1]] = ref[...]
    return scratch[0:1, :]


def dot(a, b):
    return jnp.dot(a, b, precision=EXACT, preferred_element_type=jnp.float32)


def dot_t(a, b):
    return lax.dot_general(
        a, b, (((1,), (1,)), ((), ())), precision=EXACT, preferred_element_type=jnp.float32
    )


def time_kernel(shifts, windows, time_ref, late_ref, x_ref, partial_ref, others_ref, scratch):
    shots, stations, window = x_ref.shape
    half = (time_ref.shape[1] - 1) // 2
    place = lax.axis_index("tm")
    base = window // 2
    late = band([wide(late_ref, scratch)], window, 2 * window, half - base)
    sample = place * window - base + iota((window, 2 * window), 1)
    late = jnp.where((sample >= 0) & (sample < windows * window), late, 0.0)
    taps = wide(time_ref, scratch)
    for n, shift in enumerate((lambda _: 0,) + shifts):
        matrix = dot(late, band([taps], 2 * window, window, shift(place) * window + base + half))
        if n == 0:
            own = dot_t(x_ref[...].reshape(shots * stations, window), matrix)
            partial_ref[...] = own.reshape(partial_ref.shape)
        else:
            others_ref[n - 1] = matrix


def station_kernel(order_ref, rec_ref, live_ref, partial_ref, matrix_ref, *refs):
    *halo_refs, out_ref, scratch, flags, padded, done = refs
    shots, stations, window = partial_ref.shape
    half = (rec_ref.shape[1] - 1) // 2
    flags[0:shots, :] = live_ref[...].astype(jnp.float32)
    columns = jnp.transpose(flags[...])
    edge = LANES // 2
    padded[0:edge, :] = jnp.zeros((edge, shots * window), jnp.float32)
    padded[edge + stations :, :] = jnp.zeros((edge, shots * window), jnp.float32)
    alive = [jnp.broadcast_to(columns[:, s : s + 1], (stations, window)) for s in range(shots)]
    for s in range(shots):
        total = partial_ref[s]
        for n, halo in enumerate(halo_refs):
            total = total + dot_t(halo[s], matrix_ref[n])
        padded[edge : edge + stations, s * window : (s + 1) * window] = total * alive[s]
    matrix = band([wide(rec_ref, scratch)], LANES, 2 * LANES, half - edge)
    for start in range(0, stations, LANES):
        block = dot(matrix, padded[start : start + 2 * LANES, :])
        for s in range(shots):
            done[s, start : start + LANES, :] = (
                block[:, s * window : (s + 1) * window] * alive[s][start : start + LANES]
            )
    groups, _, members, _ = out_ref.shape

    def group(g, carry):
        for q in range(members):
            station = order_ref[g * members + q]
            for s in range(shots):
                out_ref[g, s, pl.ds(q, 1), :] = done[s, pl.ds(station, 1), :]
        return carry

    lax.fori_loop(0, groups, group, 0)


def shot_matrix_kernel(half, taps_ref, out_ref):
    size = out_ref.shape[0]
    chunks = [taps_ref[q : q + 1, :] for q in range(taps_ref.shape[0])]
    out_ref[...] = band(chunks, size, size, SUBLANES * half)


def shot_kernel(matrix_ref, in_ref, out_ref):
    shots, members, window = in_ref.shape
    rows = SUBLANES * shots
    for start in range(0, members, 2 * SUBLANES):
        parts = [
            in_ref[:, a : a + SUBLANES, :].reshape(rows, window)
            for a in (start, start + SUBLANES)
        ]
        result = dot(matrix_ref[...], jnp.concatenate(parts, axis=1))
        for n, a in enumerate((start, start + SUBLANES)):
            out_ref[:, a : a + SUBLANES, :] = result[:, n * window : (n + 1) * window].reshape(
                shots, SUBLANES, window
            )


def split(value, count=3):
    pieces = []
    for _ in range(count):
        pieces.append(value.astype(jnp.bfloat16))
        if len(pieces) < count:
            value = value - pieces[-1].astype(jnp.float32)
    return pieces


def product(a, b):
    terms = ((0, 0), (1, 0), (2, 0), (0, 1), (1, 1), (0, 2))
    return sum(jnp.dot(a[i], b[j], preferred_element_type=jnp.float32) for i, j in terms)


def stacked(a, b):
    rows = a[0].shape[0]
    total = None
    for j in range(PIECES):
        left = jnp.concatenate(a[: PIECES - j], axis=0) if j < PIECES - 1 else a[0]
        terms = jnp.dot(left, b[j], preferred_element_type=jnp.float32)
        for i in range(PIECES - j):
            term = terms[i * rows : (i + 1) * rows]
            total = term if total is None else total + term
    return total


def diagonal(ref, scratch, backwards):
    count = ref.shape[1]
    lane = iota((SUBLANES, LANES), 1) - iota((SUBLANES, LANES), 0)
    used = (lane >= 0) & (lane < count)
    lane = jnp.clip(lane, 0, count - 1)
    taps = jnp.broadcast_to(wide(ref, scratch), (SUBLANES, LANES))
    taps = jnp.take_along_axis(
        taps, count - 1 - lane if backwards else lane, axis=1, mode="promise_in_bounds"
    )
    pieces = split(jnp.where(used, taps, 0.0))
    return [piece.astype(jnp.float32) for piece in pieces], count + SUBLANES - 1


def banded(diagonals, rows, cols, first, mask=None):
    pieces, wide_lanes = diagonals
    lane = iota((SUBLANES, LANES), 1)
    strips = [[] for _ in pieces]
    for row in range(0, rows, SUBLANES):
        start = row + first
        stop = start + wide_lanes
        for n, piece in enumerate(pieces):
            turned = pltpu.roll(piece, start % LANES, 1)
            tiles = []
            for low in range(0, cols, LANES):
                high = low + LANES
                if stop <= low or start >= high:
                    tiles.append(jnp.zeros((SUBLANES, LANES), jnp.float32))
                    continue
                tile = turned
                if start < low:
                    tile = jnp.where(lane < stop - low, tile, 0.0)
                elif stop > high:
                    tile = jnp.where(lane >= start - low, tile, 0.0)
                if mask is not None:
                    tile = tile * mask[:, low:high]
                tiles.append(tile)
            strips[n].append(jnp.concatenate(tiles, axis=1))
    return [jnp.concatenate(parts, axis=0).astype(jnp.bfloat16) for parts in strips]


MARGIN = 16


def spans(stations):
    step = LANES - 2 * MARGIN
    return [(start, min(step, stations - start)) for start in range(0, stations, step)]


def prepare_kernel(
    time_hbm, late_hbm, rec_hbm, shot_hbm, live_hbm, order_hbm, data_hbm, *refs
):
    times_ref, stations_ref, order_ref, own_ref, across_ref, *refs = refs
    time_ref, late_ref, rec_ref, shot_ref, live_ref, place_ref, data_ref, scratch, flags, sems = refs
    place = lax.axis_index("tm")
    stations, window = data_ref.shape
    samples = 2 * window
    half = (time_ref.shape[1] - 1) // 2
    pairs = (
        (time_hbm, time_ref),
        (late_hbm, late_ref),
        (rec_hbm, rec_ref),
        (shot_hbm, shot_ref),
        (live_hbm, live_ref),
        (order_hbm, place_ref),
        (data_hbm.at[place], data_ref),
    )
    copies = [pltpu.make_async_copy(a, b, sems.at[n]) for n, (a, b) in enumerate(pairs)]
    for copy in copies:
        copy.start()
    flags[...] = jnp.zeros_like(flags)
    for copy in copies[:6]:
        copy.wait()
    time_pieces = banded(diagonal(time_ref, scratch.at[0], True), samples, samples, -half)
    late_pieces = banded(diagonal(late_ref, scratch.at[1], True), samples, samples, -half)
    both = split(product(time_pieces, late_pieces))
    for n, piece in enumerate(both):
        for side in range(2):
            row = pl.multiple_of((place ^ side) * window, window)
            times_ref[n, pl.ds(row, window), :] = piece[side * window : (side + 1) * window, :]
    alive = live_ref[pl.ds(place, 1), :].astype(jnp.float32)
    flags[0:1, MARGIN : MARGIN + stations] = alive
    taps = diagonal(rec_ref, scratch.at[2], False)
    for m, (start, count) in enumerate(spans(stations)):
        mask = jnp.broadcast_to(flags[0:1, start : start + LANES], (SUBLANES, LANES))
        high, middle, low = banded(taps, count, LANES, MARGIN - half, mask)
        for n, pair in enumerate(((high, high), (middle, middle), (low, high))):
            for side in range(2):
                stations_ref[n, m, 0:count, side * LANES : (side + 1) * LANES] = pair[side]
    order = jnp.broadcast_to(place_ref[...].astype(jnp.float32), (SUBLANES, stations))
    order = jnp.transpose(order)[:, 0:1]
    numbers = iota((stations, stations), 1).astype(jnp.float32)
    order_ref[...] = jnp.where(numbers == order, alive, 0.0).astype(jnp.bfloat16)
    copies[6].wait()
    for n, piece in enumerate(split(data_ref[...])):
        own_ref[n] = piece
    matrix = spread_matrix(shot_ref, scratch.at[3], across_ref.shape[1] // SUBLANES)
    for n, piece in enumerate(matrix):
        across_ref[n] = piece


def sorted_kernel(times_ref, stations_ref, order_ref, own_ref, other_ref, out_ref, *refs):
    padded, done = refs
    place = lax.axis_index("tm")
    _, stations, window = other_ref.shape
    tail = padded.shape[1] - MARGIN - stations
    padded[:, 0:MARGIN, :] = jnp.zeros((PIECES, MARGIN, 2 * window), jnp.bfloat16)
    padded[:, MARGIN + stations :, :] = jnp.zeros((PIECES, tail, 2 * window), jnp.bfloat16)
    other = split(other_ref[place])
    both = [jnp.concatenate([own_ref[n], other[n]], axis=1) for n in range(PIECES)]
    times = [times_ref[n] for n in range(PIECES)]
    step = stations // 2
    for start in range(0, stations, step):
        filtered = stacked([piece[start : start + step] for piece in both], times)
        for n, piece in enumerate(split(filtered)):
            padded[n, MARGIN + start : MARGIN + start + step, :] = piece
    for m, (start, count) in enumerate(spans(stations)):
        high, middle, low = (padded[n, start : start + LANES, :] for n in range(PIECES))
        near = jnp.concatenate([high, middle], axis=0)
        far = jnp.concatenate([high, low], axis=0)
        upper = jnp.concatenate([stations_ref[n, m, 0:count, :] for n in range(2)], axis=0)
        both = jnp.dot(upper, near, preferred_element_type=jnp.float32)
        block = both[:count] + both[count:]
        lower = stations_ref[2, m, 0:count, :]
        block = block + jnp.dot(lower, far, preferred_element_type=jnp.float32)
        for n, piece in enumerate(split(block, SORTED)):
            done[n, start : start + count, :] = piece
    groups, _, members, _ = out_ref.shape
    step = groups // 2
    for first in range(0, groups, step):
        pick = order_ref[first * members : (first + step) * members, :]
        rows = sum(
            jnp.dot(pick, done[n], preferred_element_type=jnp.float32)
            for n in reversed(range(SORTED))
        )
        for side in range(2):
            out_ref[first : first + step, side] = rows[
                :, side * window : (side + 1) * window
            ].reshape(step, members, window)


def spread_matrix(ref, scratch, shots):
    count = ref.shape[1]
    half = (count - 1) // 2
    lane = iota((SUBLANES, LANES), 1)
    turn = lane - iota((SUBLANES, LANES), 0)
    taps = jnp.broadcast_to(wide(ref, scratch), (SUBLANES, LANES))
    chunks = []
    for low in range(0, SUBLANES * count, LANES):
        at = turn + low
        used = (at >= 0) & (at < SUBLANES * count) & (at & (SUBLANES - 1) == 0)
        tap = jnp.clip(at >> (SUBLANES.bit_length() - 1), 0, count - 1)
        picked = jnp.take_along_axis(taps, tap, axis=1, mode="promise_in_bounds")
        chunks.append([p.astype(jnp.float32) for p in split(jnp.where(used, picked, 0.0))])
    none = jnp.zeros((SUBLANES, LANES), jnp.float32)
    strips = [[] for _ in range(PIECES)]
    for shot in range(shots):
        start = SUBLANES * (shot - half)
        for n in range(PIECES):
            turned = [pltpu.roll(chunk[n], start % LANES, 1) for chunk in chunks]
            tiles = []
            for low in range(0, SUBLANES * shots, LANES):
                tile = none
                for q in range(len(chunks)):
                    at = start + q * LANES - low
                    if at == 0:
                        tile = turned[q]
                    elif 0 < at < LANES:
                        tile = jnp.where(lane >= at, turned[q], tile)
                    elif -LANES < at < 0:
                        tile = jnp.where(lane < at + LANES, turned[q], tile)
                tiles.append(tile)
            strips[n].append(jnp.concatenate(tiles, axis=1))
    return [jnp.concatenate(parts, axis=0).astype(jnp.bfloat16) for parts in strips]


def across_kernel(matrix_ref, in_ref, out_hbm, result, sems):
    shots, members, window = in_ref.shape
    matrix = [matrix_ref[n] for n in range(PIECES)]
    copies = []
    for start in range(0, members, 2 * SUBLANES):
        parts = [
            in_ref[:, a : a + SUBLANES, :].reshape(SUBLANES * shots, window)
            for a in (start, start + SUBLANES)
        ]
        rows = product(matrix, split(jnp.concatenate(parts, axis=1)))
        for n, a in enumerate((start, start + SUBLANES)):
            result[:, a : a + SUBLANES, :] = rows[:, n * window : (n + 1) * window].reshape(
                shots, SUBLANES, window
            )
        span = (slice(None), pl.ds(start, 2 * SUBLANES))
        copies.append(
            pltpu.make_async_copy(result.at[span], out_hbm.at[span], sems.at[len(copies)])
        )
        copies[-1].start()
    for copy in copies:
        copy.wait()


def still(array):
    return pltpu.with_memory_space_constraint(array, pltpu.HBM)


def paired(shot_data, live_mask, recv_order, rec_taps, time_taps, shot_taps, late_taps):
    shots, stations, window = shot_data.shape
    groups = lax.axis_size("shot")
    members = stations // groups
    f32, bf16 = jnp.float32, jnp.bfloat16
    row = lambda values: values.reshape(1, -1)
    samples = 2 * window
    blocks = spans(stations)
    tap_count = rec_taps.shape[0]
    grant = pltpu.CompilerParams(vmem_limit_bytes=16 * 2**20)
    traded = lax.ppermute(shot_data, "tm", [(0, 1), (1, 0)])
    taps = [row(values) for values in (time_taps, late_taps, rec_taps, shot_taps)]
    total_shots = groups * shots
    spread = SUBLANES * total_shots
    *prepared, matrix = pl.pallas_call(
        prepare_kernel,
        out_shape=[
            jax.ShapeDtypeStruct((PIECES, samples, samples), bf16),
            jax.ShapeDtypeStruct((PIECES, len(blocks), LANES - 2 * MARGIN, 2 * LANES), bf16),
            jax.ShapeDtypeStruct((stations, stations), bf16),
            jax.ShapeDtypeStruct((PIECES, stations, window), bf16),
            jax.ShapeDtypeStruct((PIECES, spread, spread), bf16),
        ],
        in_specs=[HBM] * 7,
        out_specs=[VMEM] * 5,
        scratch_shapes=[pltpu.VMEM((1, tap_count), f32)] * 4
        + [
            pltpu.VMEM((shots, stations), jnp.int32),
            pltpu.VMEM((1, stations), jnp.int32),
            pltpu.VMEM((stations, window), f32),
            pltpu.VMEM((4, SUBLANES, LANES), f32),
            pltpu.VMEM((1, blocks[-1][0] + LANES), f32),
            pltpu.SemaphoreType.DMA((7,)),
        ],
        compiler_params=grant,
        cost_estimate=pl.CostEstimate(flops=10**8, bytes_accessed=10**6, transcendentals=0),
    )(*(still(a) for a in (*taps, live_mask, row(recv_order), shot_data)))
    packed = pl.pallas_call(
        sorted_kernel,
        out_shape=jax.ShapeDtypeStruct((groups, 2, members, window), f32),
        in_specs=[VMEM] * 5,
        out_specs=VMEM,
        scratch_shapes=[
            pltpu.VMEM((PIECES, blocks[-1][0] + LANES, samples), bf16),
            pltpu.VMEM((SORTED, stations, samples), bf16),
        ],
        compiler_params=grant,
    )(*prepared, traded)
    packed = packed.reshape(groups * 2, members, window)
    moved = lax.all_to_all(packed, ("shot", "tm"), split_axis=0, concat_axis=0, tiled=True)
    return pl.pallas_call(
        across_kernel,
        out_shape=jax.ShapeDtypeStruct(moved.shape, f32),
        in_specs=[VMEM] * 2,
        out_specs=HBM,
        scratch_shapes=[
            pltpu.VMEM(moved.shape, f32),
            pltpu.SemaphoreType.DMA((members // (2 * SUBLANES),)),
        ],
        compiler_params=grant,
    )(matrix, moved)


def spread_taps(taps):
    spread = lax.pad(taps, jnp.float32(0), [(0, 0, SUBLANES - 1)])
    return jnp.pad(spread, (0, -spread.shape[0] % LANES)).reshape(-1, LANES)


def shards(shot_data, live_mask, recv_order, rec_taps, time_taps, shot_taps, late_taps):
    shots, stations, window = shot_data.shape
    windows = lax.axis_size("tm")
    groups = lax.axis_size("shot")
    if windows == 2 and shots == 2:
        return paired(
            shot_data, live_mask, recv_order, rec_taps, time_taps, shot_taps, late_taps
        )
    f32 = jnp.float32
    up = [(i, i + 1) for i in range(windows - 1)]
    down = [(j, i) for i, j in up]
    halos = [lax.ppermute(shot_data, "tm", up), lax.ppermute(shot_data, "tm", down)]
    shifts = (lambda place: -1, lambda place: 1)
    row = lambda taps: taps.reshape(1, -1)
    partial, matrices = pl.pallas_call(
        functools.partial(time_kernel, shifts, windows),
        out_shape=[
            jax.ShapeDtypeStruct((shots, stations, window), f32),
            jax.ShapeDtypeStruct((len(halos), window, window), f32),
        ],
        compiler_params=pltpu.CompilerParams(vmem_limit_bytes=32 * 2**20),
        in_specs=[VMEM] * 3,
        out_specs=[VMEM] * 2,
        scratch_shapes=[pltpu.VMEM((SUBLANES, LANES), f32)],
        cost_estimate=pl.CostEstimate(flops=10**8, bytes_accessed=10**6, transcendentals=0),
    )(row(time_taps), row(late_taps), shot_data)
    members = stations // groups
    blocks = pl.pallas_call(
        station_kernel,
        out_shape=jax.ShapeDtypeStruct((groups, shots, members, window), f32),
        compiler_params=pltpu.CompilerParams(vmem_limit_bytes=32 * 2**20),
        in_specs=[SMEM] + [VMEM] * (4 + len(halos)),
        out_specs=VMEM,
        scratch_shapes=[
            pltpu.VMEM((SUBLANES, LANES), f32),
            pltpu.VMEM((SUBLANES, stations), f32),
            pltpu.VMEM((stations + LANES, shots * window), f32),
            pltpu.VMEM((shots, stations, window), f32),
        ],
    )(recv_order, row(rec_taps), live_mask, partial, matrices, *halos)
    moved = lax.all_to_all(blocks, "shot", split_axis=0, concat_axis=0, tiled=True)
    total_shots = groups * shots
    moved = moved.reshape(total_shots, members, window)
    matrix = pl.pallas_call(
        functools.partial(shot_matrix_kernel, (shot_taps.shape[0] - 1) // 2),
        out_shape=jax.ShapeDtypeStruct((SUBLANES * total_shots, SUBLANES * total_shots), f32),
        compiler_params=pltpu.CompilerParams(vmem_limit_bytes=32 * 2**20),
        in_specs=[VMEM],
        out_specs=VMEM,
        cost_estimate=pl.CostEstimate(flops=10**6, bytes_accessed=10**6, transcendentals=0),
    )(spread_taps(shot_taps))
    return pl.pallas_call(
        shot_kernel,
        out_shape=jax.ShapeDtypeStruct(moved.shape, f32),
        compiler_params=pltpu.CompilerParams(vmem_limit_bytes=32 * 2**20),
        in_specs=[VMEM] * 2,
        out_specs=VMEM,
    )(matrix, moved)


def solution(mesh):
    placed = (P("shot", None, "tm"), P("shot", None), P(), P(), P(), P(), P())
    return jax.shard_map(
        shards, mesh=mesh, in_specs=placed, out_specs=P(None, "shot", "tm"), check_vma=False
    )
```

```python
import functools

import jax
import jax.numpy as jnp
from jax import lax
from jax.experimental import pallas as pl
from jax.experimental.pallas import tpu as pltpu
from jax.sharding import PartitionSpec as P

LANES = 128
SUBLANES = 8
PIECES = 3
SORTED = 3
EXACT = lax.Precision.HIGHEST
VMEM = pl.BlockSpec(memory_space=pltpu.VMEM)
HBM = pl.BlockSpec(memory_space=pltpu.HBM)
SMEM = pl.BlockSpec(memory_space=pltpu.SMEM)


def iota(shape, dim):
    return lax.broadcasted_iota(jnp.int32, shape, dim)


def band(chunks, rows, cols, shift):
    blocks = []
    for start in range(0, cols, LANES):
        offset = iota((rows, LANES), 1) - iota((rows, LANES), 0) + (shift + start)
        block = None
        turn = jnp.asarray(-(shift + start), jnp.int32) & (LANES - 1)
        for q, chunk in enumerate(chunks):
            first = pltpu.roll(jnp.broadcast_to(chunk, (SUBLANES, LANES)), turn, 1)
            spread = pltpu.roll(
                jnp.broadcast_to(first[:1], (rows, LANES)), 0, 1, stride=1, stride_axis=0
            )
            here = (offset >= q * LANES) & (offset < (q + 1) * LANES)
            part = jnp.where(here, spread, 0.0)
            block = part if block is None else block + part
        blocks.append(block)
    return blocks[0] if len(blocks) == 1 else jnp.concatenate(blocks, axis=1)


def wide(ref, scratch):
    scratch[...] = jnp.zeros_like(scratch)
    scratch[0:1, 0 : ref.shape[1]] = ref[...]
    return scratch[0:1, :]


def dot(a, b):
    return jnp.dot(a, b, precision=EXACT, preferred_element_type=jnp.float32)


def dot_t(a, b):
    return lax.dot_general(
        a, b, (((1,), (1,)), ((), ())), precision=EXACT, preferred_element_type=jnp.float32
    )


def time_kernel(shifts, windows, time_ref, late_ref, x_ref, partial_ref, others_ref, scratch):
    shots, stations, window = x_ref.shape
    half = (time_ref.shape[1] - 1) // 2
    place = lax.axis_index("tm")
    base = window // 2
    late = band([wide(late_ref, scratch)], window, 2 * window, half - base)
    sample = place * window - base + iota((window, 2 * window), 1)
    late = jnp.where((sample >= 0) & (sample < windows * window), late, 0.0)
    taps = wide(time_ref, scratch)
    for n, shift in enumerate((lambda _: 0,) + shifts):
        matrix = dot(late, band([taps], 2 * window, window, shift(place) * window + base + half))
        if n == 0:
            own = dot_t(x_ref[...].reshape(shots * stations, window), matrix)
            partial_ref[...] = own.reshape(partial_ref.shape)
        else:
            others_ref[n - 1] = matrix


def station_kernel(order_ref, rec_ref, live_ref, partial_ref, matrix_ref, *refs):
    *halo_refs, out_ref, scratch, flags, padded, done = refs
    shots, stations, window = partial_ref.shape
    half = (rec_ref.shape[1] - 1) // 2
    flags[0:shots, :] = live_ref[...].astype(jnp.float32)
    columns = jnp.transpose(flags[...])
    edge = LANES // 2
    padded[0:edge, :] = jnp.zeros((edge, shots * window), jnp.float32)
    padded[edge + stations :, :] = jnp.zeros((edge, shots * window), jnp.float32)
    alive = [jnp.broadcast_to(columns[:, s : s + 1], (stations, window)) for s in range(shots)]
    for s in range(shots):
        total = partial_ref[s]
        for n, halo in enumerate(halo_refs):
            total = total + dot_t(halo[s], matrix_ref[n])
        padded[edge : edge + stations, s * window : (s + 1) * window] = total * alive[s]
    matrix = band([wide(rec_ref, scratch)], LANES, 2 * LANES, half - edge)
    for start in range(0, stations, LANES):
        block = dot(matrix, padded[start : start + 2 * LANES, :])
        for s in range(shots):
            done[s, start : start + LANES, :] = (
                block[:, s * window : (s + 1) * window] * alive[s][start : start + LANES]
            )
    groups, _, members, _ = out_ref.shape

    def group(g, carry):
        for q in range(members):
            station = order_ref[g * members + q]
            for s in range(shots):
                out_ref[g, s, pl.ds(q, 1), :] = done[s, pl.ds(station, 1), :]
        return carry

    lax.fori_loop(0, groups, group, 0)


def shot_matrix_kernel(half, taps_ref, out_ref):
    size = out_ref.shape[0]
    chunks = [taps_ref[q : q + 1, :] for q in range(taps_ref.shape[0])]
    out_ref[...] = band(chunks, size, size, SUBLANES * half)


def shot_kernel(matrix_ref, in_ref, out_ref):
    shots, members, window = in_ref.shape
    rows = SUBLANES * shots
    for start in range(0, members, 2 * SUBLANES):
        parts = [
            in_ref[:, a : a + SUBLANES, :].reshape(rows, window)
            for a in (start, start + SUBLANES)
        ]
        result = dot(matrix_ref[...], jnp.concatenate(parts, axis=1))
        for n, a in enumerate((start, start + SUBLANES)):
            out_ref[:, a : a + SUBLANES, :] = result[:, n * window : (n + 1) * window].reshape(
                shots, SUBLANES, window
            )


def split(value, count=3):
    pieces = []
    for _ in range(count):
        pieces.append(value.astype(jnp.bfloat16))
        if len(pieces) < count:
            value = value - pieces[-1].astype(jnp.float32)
    return pieces


def product(a, b):
    terms = ((0, 0), (1, 0), (2, 0), (0, 1), (1, 1), (0, 2))
    return sum(jnp.dot(a[i], b[j], preferred_element_type=jnp.float32) for i, j in terms)


def stacked(a, b):
    rows = a[0].shape[0]
    total = None
    for j in range(PIECES):
        left = jnp.concatenate(a[: PIECES - j], axis=0) if j < PIECES - 1 else a[0]
        terms = jnp.dot(left, b[j], preferred_element_type=jnp.float32)
        for i in range(PIECES - j):
            term = terms[i * rows : (i + 1) * rows]
            total = term if total is None else total + term
    return total


def diagonal(ref, scratch, backwards):
    count = ref.shape[1]
    lane = iota((SUBLANES, LANES), 1) - iota((SUBLANES, LANES), 0)
    used = (lane >= 0) & (lane < count)
    lane = jnp.clip(lane, 0, count - 1)
    taps = jnp.broadcast_to(wide(ref, scratch), (SUBLANES, LANES))
    taps = jnp.take_along_axis(
        taps, count - 1 - lane if backwards else lane, axis=1, mode="promise_in_bounds"
    )
    pieces = split(jnp.where(used, taps, 0.0))
    return [piece.astype(jnp.float32) for piece in pieces], count + SUBLANES - 1


def banded(diagonals, rows, cols, first, mask=None):
    pieces, wide_lanes = diagonals
    lane = iota((SUBLANES, LANES), 1)
    strips = [[] for _ in pieces]
    for row in range(0, rows, SUBLANES):
        start = row + first
        stop = start + wide_lanes
        for n, piece in enumerate(pieces):
            turned = pltpu.roll(piece, start % LANES, 1)
            tiles = []
            for low in range(0, cols, LANES):
                high = low + LANES
                if stop <= low or start >= high:
                    tiles.append(jnp.zeros((SUBLANES, LANES), jnp.float32))
                    continue
                tile = turned
                if start < low:
                    tile = jnp.where(lane < stop - low, tile, 0.0)
                elif stop > high:
                    tile = jnp.where(lane >= start - low, tile, 0.0)
                if mask is not None:
                    tile = tile * mask[:, low:high]
                tiles.append(tile)
            strips[n].append(jnp.concatenate(tiles, axis=1))
    return [jnp.concatenate(parts, axis=0).astype(jnp.bfloat16) for parts in strips]


def doubled(a):
    near = jnp.concatenate([a[0], a[1]], axis=1)
    return near, near, jnp.concatenate([a[2], a[0]], axis=1)


def piled(b):
    pairs = ((b[0], b[0]), (b[1], b[1]), (b[0], b[2]))
    return [jnp.concatenate(pair, axis=0) for pair in pairs]


def packed_product(a, b):
    return sum(jnp.dot(x, y, preferred_element_type=jnp.float32) for x, y in zip(a, b))


MARGIN = 16


def spans(stations):
    step = LANES - 2 * MARGIN
    return [(start, min(step, stations - start)) for start in range(0, stations, step)]


def prepare_kernel(
    time_hbm, late_hbm, rec_hbm, shot_hbm, live_hbm, order_hbm, data_hbm, *refs
):
    times_ref, stations_ref, order_ref, own_ref, across_ref, *refs = refs
    *refs, matrix_ref = refs
    time_ref, late_ref, rec_ref, shot_ref, live_ref, place_ref, data_ref, scratch, flags, sems = refs
    place = lax.axis_index("tm")
    stations, window = data_ref.shape
    samples = 2 * window
    half = (time_ref.shape[1] - 1) // 2
    pairs = (
        (time_hbm, time_ref),
        (late_hbm, late_ref),
        (rec_hbm, rec_ref),
        (shot_hbm, shot_ref),
        (live_hbm, live_ref),
        (order_hbm, place_ref),
        (data_hbm.at[place], data_ref),
    )
    copies = [pltpu.make_async_copy(a, b, sems.at[n]) for n, (a, b) in enumerate(pairs)]
    for copy in copies:
        copy.start()
    flags[...] = jnp.zeros_like(flags)
    for copy in copies[:6]:
        copy.wait()
    time_pieces = banded(diagonal(time_ref, scratch.at[0], True), samples, samples, -half)
    late_pieces = banded(diagonal(late_ref, scratch.at[1], True), samples, samples, -half)
    for side in range(2):
        rows = slice(side * window, (side + 1) * window)
        combined = product([piece[rows] for piece in time_pieces], late_pieces)
        for n, piece in enumerate(split(combined)):
            matrix_ref[n, rows, :] = piece
    copies[6].wait()
    sides = [pl.ds(pl.multiple_of((place ^ side) * window, window), window) for side in range(2)]
    own, other = (piled([matrix_ref[n, side, :] for n in range(PIECES)]) for side in sides)
    for n, piece in enumerate(other):
        times_ref[n] = piece
    halves = [slice(start, start + stations // 2) for start in (0, stations // 2)]
    lefts = [doubled(split(data_ref[rows, :])) for rows in halves]
    for rows, left in zip(halves, lefts):
        own_ref[rows, :] = packed_product(left, own)
    alive = live_ref[pl.ds(place, 1), :].astype(jnp.float32)
    flags[0:1, MARGIN : MARGIN + stations] = alive
    taps = diagonal(rec_ref, scratch.at[2], False)
    for m, (start, count) in enumerate(spans(stations)):
        mask = jnp.broadcast_to(flags[0:1, start : start + LANES], (SUBLANES, LANES))
        high, middle, low = banded(taps, count, LANES, MARGIN - half, mask)
        for n, pair in enumerate(((high, high), (middle, middle), (low, high))):
            for side in range(2):
                stations_ref[n, m, 0:count, side * LANES : (side + 1) * LANES] = pair[side]
    order = jnp.broadcast_to(place_ref[...].astype(jnp.float32), (SUBLANES, stations))
    order = jnp.transpose(order)[:, 0:1]
    numbers = iota((stations, stations), 1).astype(jnp.float32)
    order_ref[...] = jnp.where(numbers == order, alive, 0.0).astype(jnp.bfloat16)
    matrix = spread_matrix(shot_ref, scratch.at[3], across_ref.shape[1] // SUBLANES)
    for n, piece in enumerate(matrix):
        across_ref[n] = piece


def sorted_kernel(times_ref, stations_ref, order_ref, own_ref, other_ref, out_ref, *refs):
    padded, done = refs
    place = lax.axis_index("tm")
    _, stations, window = other_ref.shape
    tail = padded.shape[1] - MARGIN - stations
    padded[:, 0:MARGIN, :] = jnp.zeros((PIECES, MARGIN, 2 * window), jnp.bfloat16)
    padded[:, MARGIN + stations :, :] = jnp.zeros((PIECES, tail, 2 * window), jnp.bfloat16)
    times = [times_ref[n] for n in range(PIECES)]
    step = stations // 2
    for start in range(0, stations, step):
        rows = slice(start, start + step)
        left = doubled(split(other_ref[place, rows, :]))
        filtered = own_ref[rows, :] + packed_product(left, times)
        for n, piece in enumerate(split(filtered)):
            padded[n, MARGIN + start : MARGIN + start + step, :] = piece
    for m, (start, count) in enumerate(spans(stations)):
        high, middle, low = (padded[n, start : start + LANES, :] for n in range(PIECES))
        near = jnp.concatenate([high, middle], axis=0)
        far = jnp.concatenate([high, low], axis=0)
        upper = jnp.concatenate([stations_ref[n, m, 0:count, :] for n in range(2)], axis=0)
        both = jnp.dot(upper, near, preferred_element_type=jnp.float32)
        block = both[:count] + both[count:]
        lower = stations_ref[2, m, 0:count, :]
        block = block + jnp.dot(lower, far, preferred_element_type=jnp.float32)
        for n, piece in enumerate(split(block, SORTED)):
            done[n, start : start + count, :] = piece
    groups, _, members, _ = out_ref.shape
    step = groups // 2
    for first in range(0, groups, step):
        pick = order_ref[first * members : (first + step) * members, :]
        rows = sum(
            jnp.dot(pick, done[n], preferred_element_type=jnp.float32)
            for n in reversed(range(SORTED))
        )
        for side in range(2):
            out_ref[first : first + step, side] = rows[
                :, side * window : (side + 1) * window
            ].reshape(step, members, window)


def spread_matrix(ref, scratch, shots):
    count = ref.shape[1]
    half = (count - 1) // 2
    lane = iota((SUBLANES, LANES), 1)
    turn = lane - iota((SUBLANES, LANES), 0)
    taps = jnp.broadcast_to(wide(ref, scratch), (SUBLANES, LANES))
    chunks = []
    for low in range(0, SUBLANES * count, LANES):
        at = turn + low
        used = (at >= 0) & (at < SUBLANES * count) & (at & (SUBLANES - 1) == 0)
        tap = jnp.clip(at >> (SUBLANES.bit_length() - 1), 0, count - 1)
        picked = jnp.take_along_axis(taps, tap, axis=1, mode="promise_in_bounds")
        chunks.append([p.astype(jnp.float32) for p in split(jnp.where(used, picked, 0.0))])
    none = jnp.zeros((SUBLANES, LANES), jnp.float32)
    strips = [[] for _ in range(PIECES)]
    for shot in range(shots):
        start = SUBLANES * (shot - half)
        for n in range(PIECES):
            turned = [pltpu.roll(chunk[n], start % LANES, 1) for chunk in chunks]
            tiles = []
            for low in range(0, SUBLANES * shots, LANES):
                tile = none
                for q in range(len(chunks)):
                    at = start + q * LANES - low
                    if at == 0:
                        tile = turned[q]
                    elif 0 < at < LANES:
                        tile = jnp.where(lane >= at, turned[q], tile)
                    elif -LANES < at < 0:
                        tile = jnp.where(lane < at + LANES, turned[q], tile)
                tiles.append(tile)
            strips[n].append(jnp.concatenate(tiles, axis=1))
    return [jnp.concatenate(parts, axis=0).astype(jnp.bfloat16) for parts in strips]


def across_kernel(matrix_ref, in_ref, out_hbm, result, sems):
    shots, members, window = in_ref.shape
    matrix = [matrix_ref[n] for n in range(PIECES)]
    copies = []
    for start in range(0, members, 2 * SUBLANES):
        parts = [
            in_ref[:, a : a + SUBLANES, :].reshape(SUBLANES * shots, window)
            for a in (start, start + SUBLANES)
        ]
        inputs = split(jnp.concatenate(parts, axis=1))
        step = shots // 2
        for first in range(0, shots, step):
            lines = slice(SUBLANES * first, SUBLANES * (first + step))
            rows = product([piece[lines] for piece in matrix], inputs)
            for n, a in enumerate((start, start + SUBLANES)):
                result[first : first + step, a : a + SUBLANES, :] = rows[
                    :, n * window : (n + 1) * window
                ].reshape(step, SUBLANES, window)
            span = (pl.ds(first, step), pl.ds(start, 2 * SUBLANES))
            copies.append(
                pltpu.make_async_copy(result.at[span], out_hbm.at[span], sems.at[len(copies)])
            )
            copies[-1].start()
    for copy in copies:
        copy.wait()


def still(array):
    return pltpu.with_memory_space_constraint(array, pltpu.HBM)


def paired(shot_data, live_mask, recv_order, rec_taps, time_taps, shot_taps, late_taps):
    shots, stations, window = shot_data.shape
    groups = lax.axis_size("shot")
    members = stations // groups
    f32, bf16 = jnp.float32, jnp.bfloat16
    row = lambda values: values.reshape(1, -1)
    samples = 2 * window
    blocks = spans(stations)
    tap_count = rec_taps.shape[0]
    grant = pltpu.CompilerParams(vmem_limit_bytes=16 * 2**20)
    traded = lax.ppermute(shot_data, "tm", [(0, 1), (1, 0)])
    taps = [row(values) for values in (time_taps, late_taps, rec_taps, shot_taps)]
    total_shots = groups * shots
    spread = SUBLANES * total_shots
    *prepared, matrix = pl.pallas_call(
        prepare_kernel,
        out_shape=[
            jax.ShapeDtypeStruct((PIECES, samples, samples), bf16),
            jax.ShapeDtypeStruct((PIECES, len(blocks), LANES - 2 * MARGIN, 2 * LANES), bf16),
            jax.ShapeDtypeStruct((stations, stations), bf16),
            jax.ShapeDtypeStruct((stations, samples), f32),
            jax.ShapeDtypeStruct((PIECES, spread, spread), bf16),
        ],
        in_specs=[HBM] * 7,
        out_specs=[VMEM] * 5,
        scratch_shapes=[pltpu.VMEM((1, tap_count), f32)] * 4
        + [
            pltpu.VMEM((shots, stations), jnp.int32),
            pltpu.VMEM((1, stations), jnp.int32),
            pltpu.VMEM((stations, window), f32),
            pltpu.VMEM((4, SUBLANES, LANES), f32),
            pltpu.VMEM((1, blocks[-1][0] + LANES), f32),
            pltpu.SemaphoreType.DMA((7,)),
            pltpu.VMEM((PIECES, samples, samples), bf16),
        ],
        compiler_params=grant,
        cost_estimate=pl.CostEstimate(flops=10**8, bytes_accessed=10**6, transcendentals=0),
    )(*(still(a) for a in (*taps, live_mask, row(recv_order), shot_data)))
    packed = pl.pallas_call(
        sorted_kernel,
        out_shape=jax.ShapeDtypeStruct((groups, 2, members, window), f32),
        in_specs=[VMEM] * 5,
        out_specs=VMEM,
        scratch_shapes=[
            pltpu.VMEM((PIECES, blocks[-1][0] + LANES, samples), bf16),
            pltpu.VMEM((SORTED, stations, samples), bf16),
        ],
        compiler_params=grant,
    )(*prepared, traded)
    packed = packed.reshape(groups * 2, members, window)
    moved = lax.all_to_all(packed, ("shot", "tm"), split_axis=0, concat_axis=0, tiled=True)
    return pl.pallas_call(
        across_kernel,
        out_shape=jax.ShapeDtypeStruct(moved.shape, f32),
        in_specs=[VMEM] * 2,
        out_specs=HBM,
        scratch_shapes=[
            pltpu.VMEM(moved.shape, f32),
            pltpu.SemaphoreType.DMA((2 * members // (2 * SUBLANES),)),
        ],
        compiler_params=grant,
    )(matrix, moved)


def spread_taps(taps):
    spread = lax.pad(taps, jnp.float32(0), [(0, 0, SUBLANES - 1)])
    return jnp.pad(spread, (0, -spread.shape[0] % LANES)).reshape(-1, LANES)


def shards(shot_data, live_mask, recv_order, rec_taps, time_taps, shot_taps, late_taps):
    shots, stations, window = shot_data.shape
    windows = lax.axis_size("tm")
    groups = lax.axis_size("shot")
    if windows == 2 and shots == 2:
        return paired(
            shot_data, live_mask, recv_order, rec_taps, time_taps, shot_taps, late_taps
        )
    f32 = jnp.float32
    up = [(i, i + 1) for i in range(windows - 1)]
    down = [(j, i) for i, j in up]
    halos = [lax.ppermute(shot_data, "tm", up), lax.ppermute(shot_data, "tm", down)]
    shifts = (lambda place: -1, lambda place: 1)
    row = lambda taps: taps.reshape(1, -1)
    partial, matrices = pl.pallas_call(
        functools.partial(time_kernel, shifts, windows),
        out_shape=[
            jax.ShapeDtypeStruct((shots, stations, window), f32),
            jax.ShapeDtypeStruct((len(halos), window, window), f32),
        ],
        compiler_params=pltpu.CompilerParams(vmem_limit_bytes=32 * 2**20),
        in_specs=[VMEM] * 3,
        out_specs=[VMEM] * 2,
        scratch_shapes=[pltpu.VMEM((SUBLANES, LANES), f32)],
        cost_estimate=pl.CostEstimate(flops=10**8, bytes_accessed=10**6, transcendentals=0),
    )(row(time_taps), row(late_taps), shot_data)
    members = stations // groups
    blocks = pl.pallas_call(
        station_kernel,
        out_shape=jax.ShapeDtypeStruct((groups, shots, members, window), f32),
        compiler_params=pltpu.CompilerParams(vmem_limit_bytes=32 * 2**20),
        in_specs=[SMEM] + [VMEM] * (4 + len(halos)),
        out_specs=VMEM,
        scratch_shapes=[
            pltpu.VMEM((SUBLANES, LANES), f32),
            pltpu.VMEM((SUBLANES, stations), f32),
            pltpu.VMEM((stations + LANES, shots * window), f32),
            pltpu.VMEM((shots, stations, window), f32),
        ],
    )(recv_order, row(rec_taps), live_mask, partial, matrices, *halos)
    moved = lax.all_to_all(blocks, "shot", split_axis=0, concat_axis=0, tiled=True)
    total_shots = groups * shots
    moved = moved.reshape(total_shots, members, window)
    matrix = pl.pallas_call(
        functools.partial(shot_matrix_kernel, (shot_taps.shape[0] - 1) // 2),
        out_shape=jax.ShapeDtypeStruct((SUBLANES * total_shots, SUBLANES * total_shots), f32),
        compiler_params=pltpu.CompilerParams(vmem_limit_bytes=32 * 2**20),
        in_specs=[VMEM],
        out_specs=VMEM,
        cost_estimate=pl.CostEstimate(flops=10**6, bytes_accessed=10**6, transcendentals=0),
    )(spread_taps(shot_taps))
    return pl.pallas_call(
        shot_kernel,
        out_shape=jax.ShapeDtypeStruct(moved.shape, f32),
        compiler_params=pltpu.CompilerParams(vmem_limit_bytes=32 * 2**20),
        in_specs=[VMEM] * 2,
        out_specs=VMEM,
    )(matrix, moved)


def solution(mesh):
    placed = (P("shot", None, "tm"), P("shot", None), P(), P(), P(), P(), P())
    return jax.shard_map(
        shards, mesh=mesh, in_specs=placed, out_specs=P(None, "shot", "tm"), check_vma=False
    )
```

```python
import functools
import math

import jax
import jax.numpy as jnp
from jax import lax
from jax.experimental import pallas as pl
from jax.experimental.pallas import tpu as pltpu
from jax.sharding import PartitionSpec as P

LANES = 128
SUBLANES = 8
PIECES = 3
SORTED = 3
EXACT = lax.Precision.HIGHEST
VMEM = pl.BlockSpec(memory_space=pltpu.VMEM)
HBM = pl.BlockSpec(memory_space=pltpu.HBM)
SMEM = pl.BlockSpec(memory_space=pltpu.SMEM)


def iota(shape, dim):
    return lax.broadcasted_iota(jnp.int32, shape, dim)


def band(chunks, rows, cols, shift):
    blocks = []
    for start in range(0, cols, LANES):
        offset = iota((rows, LANES), 1) - iota((rows, LANES), 0) + (shift + start)
        block = None
        turn = jnp.asarray(-(shift + start), jnp.int32) & (LANES - 1)
        for q, chunk in enumerate(chunks):
            first = pltpu.roll(jnp.broadcast_to(chunk, (SUBLANES, LANES)), turn, 1)
            spread = pltpu.roll(
                jnp.broadcast_to(first[:1], (rows, LANES)), 0, 1, stride=1, stride_axis=0
            )
            here = (offset >= q * LANES) & (offset < (q + 1) * LANES)
            part = jnp.where(here, spread, 0.0)
            block = part if block is None else block + part
        blocks.append(block)
    return blocks[0] if len(blocks) == 1 else jnp.concatenate(blocks, axis=1)


def wide(ref, scratch):
    scratch[...] = jnp.zeros_like(scratch)
    scratch[0:1, 0 : ref.shape[1]] = ref[...]
    return scratch[0:1, :]


def dot(a, b):
    return jnp.dot(a, b, precision=EXACT, preferred_element_type=jnp.float32)


def dot_t(a, b):
    return lax.dot_general(
        a, b, (((1,), (1,)), ((), ())), precision=EXACT, preferred_element_type=jnp.float32
    )


def time_kernel(shifts, windows, time_ref, late_ref, x_ref, partial_ref, others_ref, scratch):
    shots, stations, window = x_ref.shape
    half = (time_ref.shape[1] - 1) // 2
    place = lax.axis_index("tm")
    base = window // 2
    late = band([wide(late_ref, scratch)], window, 2 * window, half - base)
    sample = place * window - base + iota((window, 2 * window), 1)
    late = jnp.where((sample >= 0) & (sample < windows * window), late, 0.0)
    taps = wide(time_ref, scratch)
    for n, shift in enumerate((lambda _: 0,) + shifts):
        matrix = dot(late, band([taps], 2 * window, window, shift(place) * window + base + half))
        if n == 0:
            own = dot_t(x_ref[...].reshape(shots * stations, window), matrix)
            partial_ref[...] = own.reshape(partial_ref.shape)
        else:
            others_ref[n - 1] = matrix


def station_kernel(order_ref, rec_ref, live_ref, partial_ref, matrix_ref, *refs):
    *halo_refs, out_ref, scratch, flags, padded, done = refs
    shots, stations, window = partial_ref.shape
    half = (rec_ref.shape[1] - 1) // 2
    flags[0:shots, :] = live_ref[...].astype(jnp.float32)
    columns = jnp.transpose(flags[...])
    edge = LANES // 2
    padded[0:edge, :] = jnp.zeros((edge, shots * window), jnp.float32)
    padded[edge + stations :, :] = jnp.zeros((edge, shots * window), jnp.float32)
    alive = [jnp.broadcast_to(columns[:, s : s + 1], (stations, window)) for s in range(shots)]
    for s in range(shots):
        total = partial_ref[s]
        for n, halo in enumerate(halo_refs):
            total = total + dot_t(halo[s], matrix_ref[n])
        padded[edge : edge + stations, s * window : (s + 1) * window] = total * alive[s]
    matrix = band([wide(rec_ref, scratch)], LANES, 2 * LANES, half - edge)
    for start in range(0, stations, LANES):
        block = dot(matrix, padded[start : start + 2 * LANES, :])
        for s in range(shots):
            done[s, start : start + LANES, :] = (
                block[:, s * window : (s + 1) * window] * alive[s][start : start + LANES]
            )
    groups, _, members, _ = out_ref.shape

    def group(g, carry):
        for q in range(members):
            station = order_ref[g * members + q]
            for s in range(shots):
                out_ref[g, s, pl.ds(q, 1), :] = done[s, pl.ds(station, 1), :]
        return carry

    lax.fori_loop(0, groups, group, 0)


def shot_matrix_kernel(half, taps_ref, out_ref):
    size = out_ref.shape[0]
    chunks = [taps_ref[q : q + 1, :] for q in range(taps_ref.shape[0])]
    out_ref[...] = band(chunks, size, size, SUBLANES * half)


def shot_kernel(matrix_ref, in_ref, out_ref):
    shots, members, window = in_ref.shape
    rows = SUBLANES * shots
    for start in range(0, members, 2 * SUBLANES):
        parts = [
            in_ref[:, a : a + SUBLANES, :].reshape(rows, window)
            for a in (start, start + SUBLANES)
        ]
        result = dot(matrix_ref[...], jnp.concatenate(parts, axis=1))
        for n, a in enumerate((start, start + SUBLANES)):
            out_ref[:, a : a + SUBLANES, :] = result[:, n * window : (n + 1) * window].reshape(
                shots, SUBLANES, window
            )


def split(value, count=3):
    pieces = []
    for _ in range(count):
        pieces.append(value.astype(jnp.bfloat16))
        if len(pieces) < count:
            value = value - pieces[-1].astype(jnp.float32)
    return pieces


def product(a, b):
    terms = ((0, 0), (1, 0), (2, 0), (0, 1), (1, 1), (0, 2))
    return sum(jnp.dot(a[i], b[j], preferred_element_type=jnp.float32) for i, j in terms)


def stacked(a, b):
    rows = a[0].shape[0]
    total = None
    for j in range(PIECES):
        left = jnp.concatenate(a[: PIECES - j], axis=0) if j < PIECES - 1 else a[0]
        terms = jnp.dot(left, b[j], preferred_element_type=jnp.float32)
        for i in range(PIECES - j):
            term = terms[i * rows : (i + 1) * rows]
            total = term if total is None else total + term
    return total


def diagonal(ref, scratch, backwards):
    count = ref.shape[1]
    lane = iota((SUBLANES, LANES), 1) - iota((SUBLANES, LANES), 0)
    used = (lane >= 0) & (lane < count)
    lane = jnp.clip(lane, 0, count - 1)
    taps = jnp.broadcast_to(wide(ref, scratch), (SUBLANES, LANES))
    taps = jnp.take_along_axis(
        taps, count - 1 - lane if backwards else lane, axis=1, mode="promise_in_bounds"
    )
    pieces = split(jnp.where(used, taps, 0.0))
    return [piece.astype(jnp.float32) for piece in pieces], count + SUBLANES - 1


def banded(diagonals, rows, cols, first, mask=None):
    pieces, wide_lanes = diagonals
    lane = iota((SUBLANES, LANES), 1)
    strips = [[] for _ in pieces]
    for row in range(0, rows, SUBLANES):
        start = row + first
        stop = start + wide_lanes
        for n, piece in enumerate(pieces):
            turned = pltpu.roll(piece, start % LANES, 1)
            tiles = []
            for low in range(0, cols, LANES):
                high = low + LANES
                if stop <= low or start >= high:
                    tiles.append(jnp.zeros((SUBLANES, LANES), jnp.float32))
                    continue
                tile = turned
                if start < low:
                    tile = jnp.where(lane < stop - low, tile, 0.0)
                elif stop > high:
                    tile = jnp.where(lane >= start - low, tile, 0.0)
                if mask is not None:
                    tile = tile * mask[:, low:high]
                tiles.append(tile)
            strips[n].append(jnp.concatenate(tiles, axis=1))
    return [jnp.concatenate(parts, axis=0).astype(jnp.bfloat16) for parts in strips]


def doubled(a):
    near = jnp.concatenate([a[0], a[1]], axis=1)
    return near, near, jnp.concatenate([a[2], a[0]], axis=1)


def piled(b):
    pairs = ((b[0], b[0]), (b[1], b[1]), (b[0], b[2]))
    return [jnp.concatenate(pair, axis=0) for pair in pairs]


def packed_product(a, b):
    return sum(jnp.dot(x, y, preferred_element_type=jnp.float32) for x, y in zip(a, b))


MARGIN = 16


def spans(stations):
    step = LANES - 2 * MARGIN
    return [(start, min(step, stations - start)) for start in range(0, stations, step)]


def prepare_kernel(
    time_hbm, late_hbm, rec_hbm, shot_hbm, live_hbm, order_hbm, data_hbm, *refs
):
    times_ref, stations_ref, order_ref, own_ref, across_ref, *refs = refs
    *refs, matrix_ref = refs
    time_ref, late_ref, rec_ref, shot_ref, live_ref, place_ref, data_ref, scratch, flags, sems = refs
    place = lax.axis_index("tm")
    stations, window = data_ref.shape
    samples = 2 * window
    half = (time_ref.shape[1] - 1) // 2
    pairs = (
        (time_hbm, time_ref),
        (late_hbm, late_ref),
        (rec_hbm, rec_ref),
        (shot_hbm, shot_ref),
        (live_hbm, live_ref),
        (order_hbm, place_ref),
        (data_hbm.at[place], data_ref),
    )
    copies = [pltpu.make_async_copy(a, b, sems.at[n]) for n, (a, b) in enumerate(pairs)]
    for copy in copies:
        copy.start()
    flags[...] = jnp.zeros_like(flags)
    for copy in copies[:6]:
        copy.wait()
    time_pieces = banded(diagonal(time_ref, scratch.at[0], True), samples, samples, -half)
    late_pieces = banded(diagonal(late_ref, scratch.at[1], True), samples, samples, -half)
    for side in range(2):
        rows = slice(side * window, (side + 1) * window)
        combined = product([piece[rows] for piece in time_pieces], late_pieces)
        for n, piece in enumerate(split(combined)):
            matrix_ref[n, rows, :] = piece
    copies[6].wait()
    sides = [pl.ds(pl.multiple_of((place ^ side) * window, window), window) for side in range(2)]
    own, other = (piled([matrix_ref[n, side, :] for n in range(PIECES)]) for side in sides)
    for n, piece in enumerate(other):
        times_ref[n] = piece
    halves = [slice(start, start + stations // 2) for start in (0, stations // 2)]
    lefts = [doubled(split(data_ref[rows, :])) for rows in halves]
    for rows, left in zip(halves, lefts):
        own_ref[rows, :] = packed_product(left, own)
    alive = live_ref[pl.ds(place, 1), :].astype(jnp.float32)
    flags[0:1, MARGIN : MARGIN + stations] = alive
    taps = diagonal(rec_ref, scratch.at[2], False)
    for m, (start, count) in enumerate(spans(stations)):
        mask = jnp.broadcast_to(flags[0:1, start : start + LANES], (SUBLANES, LANES))
        high, middle, low = banded(taps, count, LANES, MARGIN - half, mask)
        for n, pair in enumerate(((high, high), (middle, middle), (low, high))):
            for side in range(2):
                stations_ref[n, m, 0:count, side * LANES : (side + 1) * LANES] = pair[side]
    order = jnp.broadcast_to(place_ref[...].astype(jnp.float32), (SUBLANES, stations))
    order = jnp.transpose(order)[:, 0:1]
    numbers = iota((stations, stations), 1).astype(jnp.float32)
    order_ref[...] = jnp.where(numbers == order, alive, 0.0).astype(jnp.bfloat16)
    matrix = spread_matrix(shot_ref, scratch.at[3], across_ref.shape[1] // SUBLANES)
    for n, piece in enumerate(matrix):
        across_ref[n] = piece


def sorted_kernel(slots, times_ref, stations_ref, order_ref, own_ref, other_ref, out_ref, *refs):
    padded, done = refs
    place = lax.axis_index("tm")
    _, stations, window = other_ref.shape
    tail = padded.shape[1] - MARGIN - stations
    padded[:, 0:MARGIN, :] = jnp.zeros((PIECES, MARGIN, 2 * window), jnp.bfloat16)
    padded[:, MARGIN + stations :, :] = jnp.zeros((PIECES, tail, 2 * window), jnp.bfloat16)
    times = [times_ref[n] for n in range(PIECES)]
    step = stations // 2
    for start in range(0, stations, step):
        rows = slice(start, start + step)
        left = doubled(split(other_ref[place, rows, :]))
        filtered = own_ref[rows, :] + packed_product(left, times)
        for n, piece in enumerate(split(filtered)):
            padded[n, MARGIN + start : MARGIN + start + step, :] = piece
    for m, (start, count) in enumerate(spans(stations)):
        high, middle, low = (padded[n, start : start + LANES, :] for n in range(PIECES))
        near = jnp.concatenate([high, middle], axis=0)
        far = jnp.concatenate([high, low], axis=0)
        upper = jnp.concatenate([stations_ref[n, m, 0:count, :] for n in range(2)], axis=0)
        both = jnp.dot(upper, near, preferred_element_type=jnp.float32)
        block = both[:count] + both[count:]
        lower = stations_ref[2, m, 0:count, :]
        block = block + jnp.dot(lower, far, preferred_element_type=jnp.float32)
        for n, piece in enumerate(split(block, SORTED)):
            done[n, start : start + count, :] = piece
    devices, members, _ = out_ref.shape
    groups = devices // 2
    step = groups // 2
    for first in range(0, groups, step):
        pick = order_ref[first * members : (first + step) * members, :]
        rows = sum(
            jnp.dot(pick, done[n], preferred_element_type=jnp.float32)
            for n in reversed(range(SORTED))
        )
        for group in range(step):
            lines = slice(group * members, (group + 1) * members)
            for side in range(2):
                part = rows[lines, side * window : (side + 1) * window]
                out_ref[slots[2 * (first + group) + side]] = part


def spread_matrix(ref, scratch, shots):
    count = ref.shape[1]
    half = (count - 1) // 2
    lane = iota((SUBLANES, LANES), 1)
    turn = lane - iota((SUBLANES, LANES), 0)
    taps = jnp.broadcast_to(wide(ref, scratch), (SUBLANES, LANES))
    chunks = []
    for low in range(0, SUBLANES * count, LANES):
        at = turn + low
        used = (at >= 0) & (at < SUBLANES * count) & (at & (SUBLANES - 1) == 0)
        tap = jnp.clip(at >> (SUBLANES.bit_length() - 1), 0, count - 1)
        picked = jnp.take_along_axis(taps, tap, axis=1, mode="promise_in_bounds")
        chunks.append([p.astype(jnp.float32) for p in split(jnp.where(used, picked, 0.0))])
    none = jnp.zeros((SUBLANES, LANES), jnp.float32)
    strips = [[] for _ in range(PIECES)]
    for shot in range(shots):
        start = SUBLANES * (shot - half)
        for n in range(PIECES):
            turned = [pltpu.roll(chunk[n], start % LANES, 1) for chunk in chunks]
            tiles = []
            for low in range(0, SUBLANES * shots, LANES):
                tile = none
                for q in range(len(chunks)):
                    at = start + q * LANES - low
                    if at == 0:
                        tile = turned[q]
                    elif 0 < at < LANES:
                        tile = jnp.where(lane >= at, turned[q], tile)
                    elif -LANES < at < 0:
                        tile = jnp.where(lane < at + LANES, turned[q], tile)
                tiles.append(tile)
            strips[n].append(jnp.concatenate(tiles, axis=1))
    return [jnp.concatenate(parts, axis=0).astype(jnp.bfloat16) for parts in strips]


def across_kernel(slots, matrix_ref, in_ref, out_hbm, result, sems):
    shots, members, window = in_ref.shape
    matrix = [matrix_ref[n] for n in range(PIECES)]
    copies = []
    for start in range(0, members, 2 * SUBLANES):
        parts = [
            jnp.concatenate([in_ref[slot, a : a + SUBLANES, :] for slot in slots], axis=0)
            for a in (start, start + SUBLANES)
        ]
        inputs = split(jnp.concatenate(parts, axis=1))
        step = shots // 2
        for first in range(0, shots, step):
            lines = slice(SUBLANES * first, SUBLANES * (first + step))
            rows = product([piece[lines] for piece in matrix], inputs)
            for n, a in enumerate((start, start + SUBLANES)):
                result[first : first + step, a : a + SUBLANES, :] = rows[
                    :, n * window : (n + 1) * window
                ].reshape(step, SUBLANES, window)
            span = (pl.ds(first, step), pl.ds(start, 2 * SUBLANES))
            copies.append(
                pltpu.make_async_copy(result.at[span], out_hbm.at[span], sems.at[len(copies)])
            )
            copies[-1].start()
    for copy in copies:
        copy.wait()


def still(array):
    return pltpu.with_memory_space_constraint(array, pltpu.HBM)


STRIDE = 7


def visiting_order(count):
    stride = STRIDE if math.gcd(STRIDE, count) == 1 else 1
    return [(n * stride) % count for n in range(count)]


def paired(shot_data, live_mask, recv_order, rec_taps, time_taps, shot_taps, late_taps):
    shots, stations, window = shot_data.shape
    groups = lax.axis_size("shot")
    members = stations // groups
    f32, bf16 = jnp.float32, jnp.bfloat16
    row = lambda values: values.reshape(1, -1)
    samples = 2 * window
    blocks = spans(stations)
    tap_count = rec_taps.shape[0]
    grant = pltpu.CompilerParams(vmem_limit_bytes=16 * 2**20)
    traded = lax.ppermute(shot_data, "tm", [(0, 1), (1, 0)])
    taps = [row(values) for values in (time_taps, late_taps, rec_taps, shot_taps)]
    total_shots = groups * shots
    order = visiting_order(2 * groups)
    slots = [order.index(device) for device in range(2 * groups)]
    spread = SUBLANES * total_shots
    *prepared, matrix = pl.pallas_call(
        prepare_kernel,
        out_shape=[
            jax.ShapeDtypeStruct((PIECES, samples, samples), bf16),
            jax.ShapeDtypeStruct((PIECES, len(blocks), LANES - 2 * MARGIN, 2 * LANES), bf16),
            jax.ShapeDtypeStruct((stations, stations), bf16),
            jax.ShapeDtypeStruct((stations, samples), f32),
            jax.ShapeDtypeStruct((PIECES, spread, spread), bf16),
        ],
        in_specs=[HBM] * 7,
        out_specs=[VMEM] * 5,
        scratch_shapes=[pltpu.VMEM((1, tap_count), f32)] * 4
        + [
            pltpu.VMEM((shots, stations), jnp.int32),
            pltpu.VMEM((1, stations), jnp.int32),
            pltpu.VMEM((stations, window), f32),
            pltpu.VMEM((4, SUBLANES, LANES), f32),
            pltpu.VMEM((1, blocks[-1][0] + LANES), f32),
            pltpu.SemaphoreType.DMA((7,)),
            pltpu.VMEM((PIECES, samples, samples), bf16),
        ],
        compiler_params=grant,
        cost_estimate=pl.CostEstimate(flops=10**8, bytes_accessed=10**6, transcendentals=0),
    )(*(still(a) for a in (*taps, live_mask, row(recv_order), shot_data)))
    packed = pl.pallas_call(
        functools.partial(sorted_kernel, slots),
        out_shape=jax.ShapeDtypeStruct((2 * groups, members, window), f32),
        in_specs=[VMEM] * 5,
        out_specs=VMEM,
        scratch_shapes=[
            pltpu.VMEM((PIECES, blocks[-1][0] + LANES, samples), bf16),
            pltpu.VMEM((SORTED, stations, samples), bf16),
        ],
        compiler_params=grant,
    )(*prepared, traded)
    moved = lax.all_to_all(
        packed,
        ("shot", "tm"),
        split_axis=0,
        concat_axis=0,
        tiled=True,
        axis_index_groups=[order],
    )
    return pl.pallas_call(
        functools.partial(across_kernel, slots),
        out_shape=jax.ShapeDtypeStruct(moved.shape, f32),
        in_specs=[VMEM] * 2,
        out_specs=HBM,
        scratch_shapes=[
            pltpu.VMEM(moved.shape, f32),
            pltpu.SemaphoreType.DMA((2 * members // (2 * SUBLANES),)),
        ],
        compiler_params=grant,
    )(matrix, moved)


def spread_taps(taps):
    spread = lax.pad(taps, jnp.float32(0), [(0, 0, SUBLANES - 1)])
    return jnp.pad(spread, (0, -spread.shape[0] % LANES)).reshape(-1, LANES)


def shards(shot_data, live_mask, recv_order, rec_taps, time_taps, shot_taps, late_taps):
    shots, stations, window = shot_data.shape
    windows = lax.axis_size("tm")
    groups = lax.axis_size("shot")
    if windows == 2 and shots == 2:
        return paired(
            shot_data, live_mask, recv_order, rec_taps, time_taps, shot_taps, late_taps
        )
    f32 = jnp.float32
    up = [(i, i + 1) for i in range(windows - 1)]
    down = [(j, i) for i, j in up]
    halos = [lax.ppermute(shot_data, "tm", up), lax.ppermute(shot_data, "tm", down)]
    shifts = (lambda place: -1, lambda place: 1)
    row = lambda taps: taps.reshape(1, -1)
    partial, matrices = pl.pallas_call(
        functools.partial(time_kernel, shifts, windows),
        out_shape=[
            jax.ShapeDtypeStruct((shots, stations, window), f32),
            jax.ShapeDtypeStruct((len(halos), window, window), f32),
        ],
        compiler_params=pltpu.CompilerParams(vmem_limit_bytes=32 * 2**20),
        in_specs=[VMEM] * 3,
        out_specs=[VMEM] * 2,
        scratch_shapes=[pltpu.VMEM((SUBLANES, LANES), f32)],
        cost_estimate=pl.CostEstimate(flops=10**8, bytes_accessed=10**6, transcendentals=0),
    )(row(time_taps), row(late_taps), shot_data)
    members = stations // groups
    blocks = pl.pallas_call(
        station_kernel,
        out_shape=jax.ShapeDtypeStruct((groups, shots, members, window), f32),
        compiler_params=pltpu.CompilerParams(vmem_limit_bytes=32 * 2**20),
        in_specs=[SMEM] + [VMEM] * (4 + len(halos)),
        out_specs=VMEM,
        scratch_shapes=[
            pltpu.VMEM((SUBLANES, LANES), f32),
            pltpu.VMEM((SUBLANES, stations), f32),
            pltpu.VMEM((stations + LANES, shots * window), f32),
            pltpu.VMEM((shots, stations, window), f32),
        ],
    )(recv_order, row(rec_taps), live_mask, partial, matrices, *halos)
    moved = lax.all_to_all(blocks, "shot", split_axis=0, concat_axis=0, tiled=True)
    total_shots = groups * shots
    moved = moved.reshape(total_shots, members, window)
    matrix = pl.pallas_call(
        functools.partial(shot_matrix_kernel, (shot_taps.shape[0] - 1) // 2),
        out_shape=jax.ShapeDtypeStruct((SUBLANES * total_shots, SUBLANES * total_shots), f32),
        compiler_params=pltpu.CompilerParams(vmem_limit_bytes=32 * 2**20),
        in_specs=[VMEM],
        out_specs=VMEM,
        cost_estimate=pl.CostEstimate(flops=10**6, bytes_accessed=10**6, transcendentals=0),
    )(spread_taps(shot_taps))
    return pl.pallas_call(
        shot_kernel,
        out_shape=jax.ShapeDtypeStruct(moved.shape, f32),
        compiler_params=pltpu.CompilerParams(vmem_limit_bytes=32 * 2**20),
        in_specs=[VMEM] * 2,
        out_specs=VMEM,
    )(matrix, moved)


def solution(mesh):
    placed = (P("shot", None, "tm"), P("shot", None), P(), P(), P(), P(), P())
    return jax.shard_map(
        shards, mesh=mesh, in_specs=placed, out_specs=P(None, "shot", "tm"), check_vma=False
    )
```

```python
import functools
import math

import jax
import jax.numpy as jnp
from jax import lax
from jax.experimental import pallas as pl
from jax.experimental.pallas import tpu as pltpu
from jax.sharding import PartitionSpec as P

LANES = 128
SUBLANES = 8
PIECES = 3
SORTED = 3
EXACT = lax.Precision.HIGHEST
VMEM = pl.BlockSpec(memory_space=pltpu.VMEM)
HBM = pl.BlockSpec(memory_space=pltpu.HBM)
SMEM = pl.BlockSpec(memory_space=pltpu.SMEM)


def iota(shape, dim):
    return lax.broadcasted_iota(jnp.int32, shape, dim)


def band(chunks, rows, cols, shift):
    blocks = []
    for start in range(0, cols, LANES):
        offset = iota((rows, LANES), 1) - iota((rows, LANES), 0) + (shift + start)
        block = None
        turn = jnp.asarray(-(shift + start), jnp.int32) & (LANES - 1)
        for q, chunk in enumerate(chunks):
            first = pltpu.roll(jnp.broadcast_to(chunk, (SUBLANES, LANES)), turn, 1)
            spread = pltpu.roll(
                jnp.broadcast_to(first[:1], (rows, LANES)), 0, 1, stride=1, stride_axis=0
            )
            here = (offset >= q * LANES) & (offset < (q + 1) * LANES)
            part = jnp.where(here, spread, 0.0)
            block = part if block is None else block + part
        blocks.append(block)
    return blocks[0] if len(blocks) == 1 else jnp.concatenate(blocks, axis=1)


def wide(ref, scratch):
    scratch[...] = jnp.zeros_like(scratch)
    scratch[0:1, 0 : ref.shape[1]] = ref[...]
    return scratch[0:1, :]


def dot(a, b):
    return jnp.dot(a, b, precision=EXACT, preferred_element_type=jnp.float32)


def dot_t(a, b):
    return lax.dot_general(
        a, b, (((1,), (1,)), ((), ())), precision=EXACT, preferred_element_type=jnp.float32
    )


def time_kernel(shifts, windows, time_ref, late_ref, x_ref, partial_ref, others_ref, scratch):
    shots, stations, window = x_ref.shape
    half = (time_ref.shape[1] - 1) // 2
    place = lax.axis_index("tm")
    base = window // 2
    late = band([wide(late_ref, scratch)], window, 2 * window, half - base)
    sample = place * window - base + iota((window, 2 * window), 1)
    late = jnp.where((sample >= 0) & (sample < windows * window), late, 0.0)
    taps = wide(time_ref, scratch)
    for n, shift in enumerate((lambda _: 0,) + shifts):
        matrix = dot(late, band([taps], 2 * window, window, shift(place) * window + base + half))
        if n == 0:
            own = dot_t(x_ref[...].reshape(shots * stations, window), matrix)
            partial_ref[...] = own.reshape(partial_ref.shape)
        else:
            others_ref[n - 1] = matrix


def station_kernel(order_ref, rec_ref, live_ref, partial_ref, matrix_ref, *refs):
    *halo_refs, out_ref, scratch, flags, padded, done = refs
    shots, stations, window = partial_ref.shape
    half = (rec_ref.shape[1] - 1) // 2
    flags[0:shots, :] = live_ref[...].astype(jnp.float32)
    columns = jnp.transpose(flags[...])
    edge = LANES // 2
    padded[0:edge, :] = jnp.zeros((edge, shots * window), jnp.float32)
    padded[edge + stations :, :] = jnp.zeros((edge, shots * window), jnp.float32)
    alive = [jnp.broadcast_to(columns[:, s : s + 1], (stations, window)) for s in range(shots)]
    for s in range(shots):
        total = partial_ref[s]
        for n, halo in enumerate(halo_refs):
            total = total + dot_t(halo[s], matrix_ref[n])
        padded[edge : edge + stations, s * window : (s + 1) * window] = total * alive[s]
    matrix = band([wide(rec_ref, scratch)], LANES, 2 * LANES, half - edge)
    for start in range(0, stations, LANES):
        block = dot(matrix, padded[start : start + 2 * LANES, :])
        for s in range(shots):
            done[s, start : start + LANES, :] = (
                block[:, s * window : (s + 1) * window] * alive[s][start : start + LANES]
            )
    groups, _, members, _ = out_ref.shape

    def group(g, carry):
        for q in range(members):
            station = order_ref[g * members + q]
            for s in range(shots):
                out_ref[g, s, pl.ds(q, 1), :] = done[s, pl.ds(station, 1), :]
        return carry

    lax.fori_loop(0, groups, group, 0)


def shot_matrix_kernel(half, taps_ref, out_ref):
    size = out_ref.shape[0]
    chunks = [taps_ref[q : q + 1, :] for q in range(taps_ref.shape[0])]
    out_ref[...] = band(chunks, size, size, SUBLANES * half)


def shot_kernel(matrix_ref, in_ref, out_ref):
    shots, members, window = in_ref.shape
    rows = SUBLANES * shots
    for start in range(0, members, 2 * SUBLANES):
        parts = [
            in_ref[:, a : a + SUBLANES, :].reshape(rows, window)
            for a in (start, start + SUBLANES)
        ]
        result = dot(matrix_ref[...], jnp.concatenate(parts, axis=1))
        for n, a in enumerate((start, start + SUBLANES)):
            out_ref[:, a : a + SUBLANES, :] = result[:, n * window : (n + 1) * window].reshape(
                shots, SUBLANES, window
            )


def split(value, count=3):
    pieces = []
    for _ in range(count):
        pieces.append(value.astype(jnp.bfloat16))
        if len(pieces) < count:
            value = value - pieces[-1].astype(jnp.float32)
    return pieces


def product(a, b):
    terms = ((0, 0), (1, 0), (2, 0), (0, 1), (1, 1), (0, 2))
    return sum(jnp.dot(a[i], b[j], preferred_element_type=jnp.float32) for i, j in terms)


def stacked(a, b):
    rows = a[0].shape[0]
    total = None
    for j in range(PIECES):
        left = jnp.concatenate(a[: PIECES - j], axis=0) if j < PIECES - 1 else a[0]
        terms = jnp.dot(left, b[j], preferred_element_type=jnp.float32)
        for i in range(PIECES - j):
            term = terms[i * rows : (i + 1) * rows]
            total = term if total is None else total + term
    return total


def diagonal(ref, scratch, backwards):
    count = ref.shape[1]
    lane = iota((SUBLANES, LANES), 1) - iota((SUBLANES, LANES), 0)
    used = (lane >= 0) & (lane < count)
    lane = jnp.clip(lane, 0, count - 1)
    taps = jnp.broadcast_to(wide(ref, scratch), (SUBLANES, LANES))
    taps = jnp.take_along_axis(
        taps, count - 1 - lane if backwards else lane, axis=1, mode="promise_in_bounds"
    )
    pieces = split(jnp.where(used, taps, 0.0))
    return [piece.astype(jnp.float32) for piece in pieces], count + SUBLANES - 1


def banded(diagonals, rows, cols, first, mask=None):
    pieces, wide_lanes = diagonals
    lane = iota((SUBLANES, LANES), 1)
    strips = [[] for _ in pieces]
    for row in range(0, rows, SUBLANES):
        start = row + first
        stop = start + wide_lanes
        for n, piece in enumerate(pieces):
            turned = pltpu.roll(piece, start % LANES, 1)
            tiles = []
            for low in range(0, cols, LANES):
                high = low + LANES
                if stop <= low or start >= high:
                    tiles.append(jnp.zeros((SUBLANES, LANES), jnp.float32))
                    continue
                tile = turned
                if start < low:
                    tile = jnp.where(lane < stop - low, tile, 0.0)
                elif stop > high:
                    tile = jnp.where(lane >= start - low, tile, 0.0)
                if mask is not None:
                    tile = tile * mask[:, low:high]
                tiles.append(tile)
            strips[n].append(jnp.concatenate(tiles, axis=1))
    return [jnp.concatenate(parts, axis=0).astype(jnp.bfloat16) for parts in strips]


def doubled(a):
    near = jnp.concatenate([a[0], a[1]], axis=1)
    return near, near, jnp.concatenate([a[2], a[0]], axis=1)


def piled(b):
    pairs = ((b[0], b[0]), (b[1], b[1]), (b[0], b[2]))
    return [jnp.concatenate(pair, axis=0) for pair in pairs]


def packed_product(a, b):
    return sum(jnp.dot(x, y, preferred_element_type=jnp.float32) for x, y in zip(a, b))


MARGIN = 16


def spans(stations):
    step = LANES - 2 * MARGIN
    return [(start, min(step, stations - start)) for start in range(0, stations, step)]


def prepare_kernel(
    time_hbm, late_hbm, rec_hbm, shot_hbm, live_hbm, order_hbm, data_hbm, *refs
):
    times_ref, stations_ref, order_ref, alive_ref, own_ref, across_ref, *refs = refs
    *refs, matrix_ref = refs
    time_ref, late_ref, rec_ref, shot_ref, live_ref, place_ref, data_ref, scratch, flags, sems = refs
    place = lax.axis_index("tm")
    stations, window = data_ref.shape
    samples = 2 * window
    half = (time_ref.shape[1] - 1) // 2
    pairs = (
        (time_hbm, time_ref),
        (late_hbm, late_ref),
        (rec_hbm, rec_ref),
        (shot_hbm, shot_ref),
        (live_hbm, live_ref),
        (order_hbm, place_ref),
        (data_hbm.at[place], data_ref),
    )
    copies = [pltpu.make_async_copy(a, b, sems.at[n]) for n, (a, b) in enumerate(pairs)]
    for copy in copies:
        copy.start()
    flags[...] = jnp.zeros_like(flags)
    for copy in copies[:6]:
        copy.wait()
    time_pieces = banded(diagonal(time_ref, scratch.at[0], True), samples, samples, -half)
    late_pieces = banded(diagonal(late_ref, scratch.at[1], True), samples, samples, -half)
    for side in range(2):
        rows = slice(side * window, (side + 1) * window)
        combined = product([piece[rows] for piece in time_pieces], late_pieces)
        for n, piece in enumerate(split(combined)):
            matrix_ref[n, rows, :] = piece
    copies[6].wait()
    sides = [pl.ds(pl.multiple_of((place ^ side) * window, window), window) for side in range(2)]
    own, other = (piled([matrix_ref[n, side, :] for n in range(PIECES)]) for side in sides)
    for n, piece in enumerate(other):
        times_ref[n] = piece
    halves = [slice(start, start + stations // 2) for start in (0, stations // 2)]
    lefts = [doubled(split(data_ref[rows, :])) for rows in halves]
    for rows, left in zip(halves, lefts):
        own_ref[rows, :] = packed_product(left, own)
    alive = live_ref[pl.ds(place, 1), :].astype(jnp.float32)
    flags[0:1, MARGIN : MARGIN + stations] = alive
    taps = diagonal(rec_ref, scratch.at[2], False)
    for m, (start, count) in enumerate(spans(stations)):
        mask = jnp.broadcast_to(flags[0:1, start : start + LANES], (SUBLANES, LANES))
        high, middle, low = banded(taps, count, LANES, MARGIN - half, mask)
        for n, pair in enumerate(((high, high), (middle, middle), (low, high))):
            for side in range(2):
                stations_ref[n, m, 0:count, side * LANES : (side + 1) * LANES] = pair[side]
    order = jnp.broadcast_to(place_ref[...].astype(jnp.float32), (SUBLANES, stations))
    order_ref[...] = jnp.broadcast_to(jnp.transpose(order)[:, 0:1], order_ref.shape)
    alive_ref[...] = jnp.broadcast_to(alive, alive_ref.shape)
    matrix = spread_matrix(shot_ref, scratch.at[3], across_ref.shape[1] // SUBLANES)
    for n, piece in enumerate(matrix):
        across_ref[n] = piece


def chosen(order, alive):
    lane = iota(order.shape, 1).astype(jnp.float32)
    tiles = [
        jnp.where(order == lane + float(low), alive[0:1, low : low + LANES], 0.0)
        for low in range(0, alive.shape[1], LANES)
    ]
    return jnp.concatenate(tiles, axis=1).astype(jnp.bfloat16)


def sorted_kernel(slots, times_ref, stations_ref, order_ref, alive_ref, own_ref, other_ref, out_ref, *refs):
    padded, done = refs
    place = lax.axis_index("tm")
    _, stations, window = other_ref.shape
    tail = padded.shape[1] - MARGIN - stations
    padded[:, 0:MARGIN, :] = jnp.zeros((PIECES, MARGIN, 2 * window), jnp.bfloat16)
    padded[:, MARGIN + stations :, :] = jnp.zeros((PIECES, tail, 2 * window), jnp.bfloat16)
    times = [times_ref[n] for n in range(PIECES)]
    step = stations // 2
    picks = [
        chosen(order_ref[start : start + step, :], alive_ref[...])
        for start in range(0, stations, step)
    ]
    for start in range(0, stations, step):
        rows = slice(start, start + step)
        left = doubled(split(other_ref[place, rows, :]))
        filtered = own_ref[rows, :] + packed_product(left, times)
        for n, piece in enumerate(split(filtered)):
            padded[n, MARGIN + start : MARGIN + start + step, :] = piece
    for m, (start, count) in enumerate(spans(stations)):
        high, middle, low = (padded[n, start : start + LANES, :] for n in range(PIECES))
        near = jnp.concatenate([high, middle], axis=0)
        far = jnp.concatenate([high, low], axis=0)
        upper = jnp.concatenate([stations_ref[n, m, 0:count, :] for n in range(2)], axis=0)
        both = jnp.dot(upper, near, preferred_element_type=jnp.float32)
        block = both[:count] + both[count:]
        lower = stations_ref[2, m, 0:count, :]
        block = block + jnp.dot(lower, far, preferred_element_type=jnp.float32)
        for n, piece in enumerate(split(block, SORTED)):
            done[n, start : start + count, :] = piece
    devices, members, _ = out_ref.shape
    groups = devices // 2
    step = groups // 2
    for first in range(0, groups, step):
        pick = picks[first // step]
        rows = sum(
            jnp.dot(pick, done[n], preferred_element_type=jnp.float32)
            for n in reversed(range(SORTED))
        )
        for group in range(step):
            lines = slice(group * members, (group + 1) * members)
            for side in range(2):
                part = rows[lines, side * window : (side + 1) * window]
                out_ref[slots[2 * (first + group) + side]] = part


def spread_matrix(ref, scratch, shots):
    count = ref.shape[1]
    half = (count - 1) // 2
    lane = iota((SUBLANES, LANES), 1)
    turn = lane - iota((SUBLANES, LANES), 0)
    taps = jnp.broadcast_to(wide(ref, scratch), (SUBLANES, LANES))
    chunks = []
    for low in range(0, SUBLANES * count, LANES):
        at = turn + low
        used = (at >= 0) & (at < SUBLANES * count) & (at & (SUBLANES - 1) == 0)
        tap = jnp.clip(at >> (SUBLANES.bit_length() - 1), 0, count - 1)
        picked = jnp.take_along_axis(taps, tap, axis=1, mode="promise_in_bounds")
        chunks.append([p.astype(jnp.float32) for p in split(jnp.where(used, picked, 0.0))])
    none = jnp.zeros((SUBLANES, LANES), jnp.float32)
    strips = [[] for _ in range(PIECES)]
    for shot in range(shots):
        start = SUBLANES * (shot - half)
        for n in range(PIECES):
            turned = [pltpu.roll(chunk[n], start % LANES, 1) for chunk in chunks]
            tiles = []
            for low in range(0, SUBLANES * shots, LANES):
                tile = none
                for q in range(len(chunks)):
                    at = start + q * LANES - low
                    if at == 0:
                        tile = turned[q]
                    elif 0 < at < LANES:
                        tile = jnp.where(lane >= at, turned[q], tile)
                    elif -LANES < at < 0:
                        tile = jnp.where(lane < at + LANES, turned[q], tile)
                tiles.append(tile)
            strips[n].append(jnp.concatenate(tiles, axis=1))
    return [jnp.concatenate(parts, axis=0).astype(jnp.bfloat16) for parts in strips]


def across_kernel(slots, matrix_ref, in_ref, out_hbm, result, sems):
    shots, members, window = in_ref.shape
    matrix = [matrix_ref[n] for n in range(PIECES)]
    copies = []
    for start in range(0, members, 2 * SUBLANES):
        parts = [
            jnp.concatenate([in_ref[slot, a : a + SUBLANES, :] for slot in slots], axis=0)
            for a in (start, start + SUBLANES)
        ]
        inputs = split(jnp.concatenate(parts, axis=1))
        step = shots // 2
        for first in range(0, shots, step):
            lines = slice(SUBLANES * first, SUBLANES * (first + step))
            rows = product([piece[lines] for piece in matrix], inputs)
            for n, a in enumerate((start, start + SUBLANES)):
                result[first : first + step, a : a + SUBLANES, :] = rows[
                    :, n * window : (n + 1) * window
                ].reshape(step, SUBLANES, window)
            span = (pl.ds(first, step), pl.ds(start, 2 * SUBLANES))
            copies.append(
                pltpu.make_async_copy(result.at[span], out_hbm.at[span], sems.at[len(copies)])
            )
            copies[-1].start()
    for copy in copies:
        copy.wait()


def still(array):
    return pltpu.with_memory_space_constraint(array, pltpu.HBM)


STRIDE = 7


def visiting_order(count):
    stride = STRIDE if math.gcd(STRIDE, count) == 1 else 1
    return [(n * stride) % count for n in range(count)]


def paired(shot_data, live_mask, recv_order, rec_taps, time_taps, shot_taps, late_taps):
    shots, stations, window = shot_data.shape
    groups = lax.axis_size("shot")
    members = stations // groups
    f32, bf16 = jnp.float32, jnp.bfloat16
    row = lambda values: values.reshape(1, -1)
    samples = 2 * window
    blocks = spans(stations)
    tap_count = rec_taps.shape[0]
    grant = pltpu.CompilerParams(vmem_limit_bytes=16 * 2**20)
    traded = lax.ppermute(shot_data, "tm", [(0, 1), (1, 0)])
    taps = [row(values) for values in (time_taps, late_taps, rec_taps, shot_taps)]
    total_shots = groups * shots
    order = visiting_order(2 * groups)
    slots = [order.index(device) for device in range(2 * groups)]
    spread = SUBLANES * total_shots
    *prepared, matrix = pl.pallas_call(
        prepare_kernel,
        out_shape=[
            jax.ShapeDtypeStruct((PIECES, samples, samples), bf16),
            jax.ShapeDtypeStruct((PIECES, len(blocks), LANES - 2 * MARGIN, 2 * LANES), bf16),
            jax.ShapeDtypeStruct((stations, LANES), f32),
            jax.ShapeDtypeStruct((SUBLANES, stations), f32),
            jax.ShapeDtypeStruct((stations, samples), f32),
            jax.ShapeDtypeStruct((PIECES, spread, spread), bf16),
        ],
        in_specs=[HBM] * 7,
        out_specs=[VMEM] * 6,
        scratch_shapes=[pltpu.VMEM((1, tap_count), f32)] * 4
        + [
            pltpu.VMEM((shots, stations), jnp.int32),
            pltpu.VMEM((1, stations), jnp.int32),
            pltpu.VMEM((stations, window), f32),
            pltpu.VMEM((4, SUBLANES, LANES), f32),
            pltpu.VMEM((1, blocks[-1][0] + LANES), f32),
            pltpu.SemaphoreType.DMA((7,)),
            pltpu.VMEM((PIECES, samples, samples), bf16),
        ],
        compiler_params=grant,
        cost_estimate=pl.CostEstimate(flops=10**8, bytes_accessed=10**6, transcendentals=0),
    )(*(still(a) for a in (*taps, live_mask, row(recv_order), shot_data)))
    packed = pl.pallas_call(
        functools.partial(sorted_kernel, slots),
        out_shape=jax.ShapeDtypeStruct((2 * groups, members, window), f32),
        in_specs=[VMEM] * 6,
        out_specs=VMEM,
        scratch_shapes=[
            pltpu.VMEM((PIECES, blocks[-1][0] + LANES, samples), bf16),
            pltpu.VMEM((SORTED, stations, samples), bf16),
        ],
        compiler_params=grant,
    )(*prepared, traded)
    moved = lax.all_to_all(
        packed,
        ("shot", "tm"),
        split_axis=0,
        concat_axis=0,
        tiled=True,
        axis_index_groups=[order],
    )
    return pl.pallas_call(
        functools.partial(across_kernel, slots),
        out_shape=jax.ShapeDtypeStruct(moved.shape, f32),
        in_specs=[VMEM] * 2,
        out_specs=HBM,
        scratch_shapes=[
            pltpu.VMEM(moved.shape, f32),
            pltpu.SemaphoreType.DMA((2 * members // (2 * SUBLANES),)),
        ],
        compiler_params=grant,
    )(matrix, moved)


def spread_taps(taps):
    spread = lax.pad(taps, jnp.float32(0), [(0, 0, SUBLANES - 1)])
    return jnp.pad(spread, (0, -spread.shape[0] % LANES)).reshape(-1, LANES)


def shards(shot_data, live_mask, recv_order, rec_taps, time_taps, shot_taps, late_taps):
    shots, stations, window = shot_data.shape
    windows = lax.axis_size("tm")
    groups = lax.axis_size("shot")
    if windows == 2 and shots == 2:
        return paired(
            shot_data, live_mask, recv_order, rec_taps, time_taps, shot_taps, late_taps
        )
    f32 = jnp.float32
    up = [(i, i + 1) for i in range(windows - 1)]
    down = [(j, i) for i, j in up]
    halos = [lax.ppermute(shot_data, "tm", up), lax.ppermute(shot_data, "tm", down)]
    shifts = (lambda place: -1, lambda place: 1)
    row = lambda taps: taps.reshape(1, -1)
    partial, matrices = pl.pallas_call(
        functools.partial(time_kernel, shifts, windows),
        out_shape=[
            jax.ShapeDtypeStruct((shots, stations, window), f32),
            jax.ShapeDtypeStruct((len(halos), window, window), f32),
        ],
        compiler_params=pltpu.CompilerParams(vmem_limit_bytes=32 * 2**20),
        in_specs=[VMEM] * 3,
        out_specs=[VMEM] * 2,
        scratch_shapes=[pltpu.VMEM((SUBLANES, LANES), f32)],
        cost_estimate=pl.CostEstimate(flops=10**8, bytes_accessed=10**6, transcendentals=0),
    )(row(time_taps), row(late_taps), shot_data)
    members = stations // groups
    blocks = pl.pallas_call(
        station_kernel,
        out_shape=jax.ShapeDtypeStruct((groups, shots, members, window), f32),
        compiler_params=pltpu.CompilerParams(vmem_limit_bytes=32 * 2**20),
        in_specs=[SMEM] + [VMEM] * (4 + len(halos)),
        out_specs=VMEM,
        scratch_shapes=[
            pltpu.VMEM((SUBLANES, LANES), f32),
            pltpu.VMEM((SUBLANES, stations), f32),
            pltpu.VMEM((stations + LANES, shots * window), f32),
            pltpu.VMEM((shots, stations, window), f32),
        ],
    )(recv_order, row(rec_taps), live_mask, partial, matrices, *halos)
    moved = lax.all_to_all(blocks, "shot", split_axis=0, concat_axis=0, tiled=True)
    total_shots = groups * shots
    moved = moved.reshape(total_shots, members, window)
    matrix = pl.pallas_call(
        functools.partial(shot_matrix_kernel, (shot_taps.shape[0] - 1) // 2),
        out_shape=jax.ShapeDtypeStruct((SUBLANES * total_shots, SUBLANES * total_shots), f32),
        compiler_params=pltpu.CompilerParams(vmem_limit_bytes=32 * 2**20),
        in_specs=[VMEM],
        out_specs=VMEM,
        cost_estimate=pl.CostEstimate(flops=10**6, bytes_accessed=10**6, transcendentals=0),
    )(spread_taps(shot_taps))
    return pl.pallas_call(
        shot_kernel,
        out_shape=jax.ShapeDtypeStruct(moved.shape, f32),
        compiler_params=pltpu.CompilerParams(vmem_limit_bytes=32 * 2**20),
        in_specs=[VMEM] * 2,
        out_specs=VMEM,
    )(matrix, moved)


def solution(mesh):
    placed = (P("shot", None, "tm"), P("shot", None), P(), P(), P(), P(), P())
    return jax.shard_map(
        shards, mesh=mesh, in_specs=placed, out_specs=P(None, "shot", "tm"), check_vma=False
    )
```
